512 devices in a mesh: ctx: 64 (over z, x, core), tp: 8 (over y).
Axes of the slice: x: 4, y: 8, z: 8, core: 2. Of those that a mesh axis runs over, the one named last changes fastest.
Arguments:
- queries: bfloat16 [16384, 8192], P('ctx', 'tp'), may hold values from -6 to 6
- key_vectors: bfloat16 [16384, 1024], P(('ctx', 'tp')), may hold values from -6 to 6
- value_vectors: bfloat16 [16384, 1024], P(('ctx', 'tp')), may hold values from -6 to 6
- output_gradient: bfloat16 [16384, 8192], P('ctx', 'tp'), may hold values from -6 to 6
- doc_lengths: int32 [32], replicated, may hold values from 1 to 1793, 16384 in all
Outputs:
- attn_output: bfloat16 [16384, 8192], P('ctx', 'tp')
- grad_queries: bfloat16 [16384, 8192], P('ctx', 'tp')
- key_gradient: bfloat16 [16384, 1024], P(('ctx', 'tp'))
- value_gradient: bfloat16 [16384, 1024], P(('ctx', 'tp'))
The draws below stay inside these ranges and needn't reach their ends.
All inputs are finite; a program needn't handle non-finite values.
Results may differ from the reference program's by a relative error of at most 0.02.
Values may be sent and summed in bfloat16 or wider, within the bound.
A program may use at most 64 MiB of HBM per device.

```python
import math
from functools import partial
import jax
import jax.numpy as jnp
import numpy as np
from jax import lax

QUERY_HEADS = 64
KEY_VALUE_HEADS = 8
HEAD_SIZE = 128
CONTEXT_TOKENS = 256
WINDOW = 8
PACKED_TOKENS = 16384
DOC_MAX = 1793
NDOCS = 32
N_CTX = 64


def draw_key_vectors(key, part):
    local_key_block = jax.random.fold_in(key, 11)
    unpadded_result = jnp.clip(jax.random.normal(local_key_block, (PACKED_TOKENS, KEY_VALUE_HEADS, HEAD_SIZE), jnp.float32), -6.0, 6.0)
    return unpadded_result.reshape(PACKED_TOKENS, KEY_VALUE_HEADS * HEAD_SIZE).astype(jnp.bfloat16)


def draw_queries(key, part):
    local_key_block = jax.random.fold_in(key, 23)
    heads_per_group = QUERY_HEADS // KEY_VALUE_HEADS
    unpadded_result = jnp.clip(jax.random.normal(local_key_block, (PACKED_TOKENS, KEY_VALUE_HEADS, heads_per_group, HEAD_SIZE), jnp.float32), -6.0, 6.0)
    return unpadded_result.reshape(PACKED_TOKENS, QUERY_HEADS * HEAD_SIZE).astype(jnp.bfloat16)


def block_scale(rng, shape, shards, least, high):
    loudness, own = 1.0, jax.random.fold_in(rng, 6)
    for dim, shards_of in shards:
        draws = jnp.exp(jax.random.uniform(jax.random.fold_in(own, dim), (shards_of,), jnp.float32, least / len(shards), high / len(shards)))
        loudness = loudness * jnp.repeat(draws, shape[dim] // shards_of).reshape([-1 if axis == dim else 1 for axis in range(len(shape))])
    return loudness


def split_up(number_of, total, bound, skew):
    loads = [(1 << 20) // math.isqrt(standing ** skew) + 1 for standing in range(2, number_of + 1)]
    rest, holding = total - bound - (number_of - 1), [1] * (number_of - 1)
    while rest > 0:
        candidates = [i for i in range(number_of - 1) if holding[i] < bound]
        mass, remaining = sum([loads[i] for i in candidates]), rest
        for i in candidates:
            addition = min(bound - holding[i], max(1, remaining * loads[i] // mass), rest)
            holding[i] = holding[i] + addition
            rest = rest - addition
    return np.array([bound] + holding)


def ragged_sizes(rng, amount, total, bound, skew):
    if amount == 2:
        one = jax.random.randint(rng, (), max(1, total - bound), min(bound, total - 1) + 1)
        return jnp.stack([one, total - one])
    lengths = jnp.asarray(split_up(amount, total, bound, skew), jnp.int32)
    couples = (amount - 1) // 2
    source_of, sink = lengths[1:1 + 2 * couples:2], lengths[2:2 + 2 * couples:2]
    slack = jnp.minimum(source_of - 1, bound - sink)
    moved = jax.random.randint(jax.random.fold_in(rng, 1), (couples,), 0, 1 << 20) % (slack + 1)
    lengths = lengths.at[1:1 + 2 * couples:2].set(source_of - moved).at[2:2 + 2 * couples:2].set(sink + moved)
    return lengths[jax.random.permutation(jax.random.fold_in(rng, 2), amount)]


def bell_draw(own_key, shape, scale, reach, shards=(), kind=jnp.bfloat16):
    factor_of = block_scale(own_key, shape, shards, -0.22, 0.18) if shards else 1.0
    result = jax.random.normal(own_key, shape, jnp.float32) * scale * factor_of
    return jnp.minimum(jnp.maximum(result, -reach), reach).astype(kind)


def setup_inputs(seed: int = 0) -> dict:
    streams_of = jax.random.split(jax.random.key(seed), 6)
    return {
        "queries": draw_queries(jax.random.fold_in(streams_of[5], 71), 0),
        "key_vectors": draw_key_vectors(jax.random.fold_in(streams_of[5], 71), 0),
        "value_vectors": bell_draw(streams_of[2], (PACKED_TOKENS, KEY_VALUE_HEADS * HEAD_SIZE), 1.0, 6.0, ((0, 512),)),
        "output_gradient": bell_draw(streams_of[3], (PACKED_TOKENS, QUERY_HEADS * HEAD_SIZE), 1.0, 6.0, ((0, 64), (1, 8))),
        "doc_lengths": ragged_sizes(streams_of[4], NDOCS, PACKED_TOKENS, DOC_MAX, 2).astype(jnp.int32),
    }


def doc_index_of(positions, doc_starts):
    above = (positions[:, None] >= doc_starts[None, :]).astype(jnp.int32)
    return lax.optimization_barrier(jnp.sum(above, axis=1)).astype(jnp.int32) - 1

def attend_all(block_q, block_g, key_block, value_block, allowed, score_scale):
    query_f = block_q.astype(jnp.float32)
    grad_f = block_g.astype(jnp.float32)
    key_f = key_block.astype(jnp.float32)
    value_f = value_block.astype(jnp.float32)
    scores = jnp.einsum('tgjd,kgd->gjtk', query_f, key_f) * score_scale
    scores = jnp.where(allowed[None, None], scores, -1e+30)
    row_top = lax.optimization_barrier(jnp.max(scores, axis=3, keepdims=True))
    row_total = lax.optimization_barrier(jnp.sum(jnp.exp(scores - row_top), axis=3, keepdims=True))
    log_total = row_top + jnp.log(row_total)
    weights = jnp.exp(scores - log_total)
    weights_low = weights.astype(jnp.bfloat16)
    low_f = weights_low.astype(jnp.float32)
    output = jnp.einsum('gjtk,kgd->tgjd', low_f, value_f).astype(jnp.bfloat16)
    row_delta = lax.optimization_barrier(jnp.sum(output.astype(jnp.float32) * grad_f, axis=3))
    row_delta = jnp.transpose(row_delta, (1, 2, 0))[..., None]
    grad_weights = jnp.einsum('tgjd,kgd->gjtk', grad_f, value_f)
    grad_scores = (weights * (grad_weights - row_delta) * score_scale).astype(jnp.bfloat16)
    scores_f = grad_scores.astype(jnp.float32)
    grad_query = jnp.einsum('gjtk,kgd->tgjd', scores_f, key_f).astype(jnp.bfloat16)
    grad_key = jnp.einsum('gjtk,tgjd->kgd', scores_f, query_f)
    grad_value = jnp.einsum('gjtk,tgjd->kgd', low_f, grad_f)
    return (output, grad_query, grad_key, grad_value)

def reference(queries, key_vectors, value_vectors, output_gradient, doc_lengths):
    heads_per_group = QUERY_HEADS // KEY_VALUE_HEADS
    score_scale = 1.0 / math.sqrt(HEAD_SIZE)
    reshaped_query = queries.reshape(N_CTX, CONTEXT_TOKENS, KEY_VALUE_HEADS, heads_per_group, HEAD_SIZE)
    reshaped_gradient = output_gradient.reshape(N_CTX, CONTEXT_TOKENS, KEY_VALUE_HEADS, heads_per_group, HEAD_SIZE)
    leading_rows = (WINDOW - 1) * CONTEXT_TOKENS
    key_padded = jnp.concatenate([jnp.zeros((leading_rows, KEY_VALUE_HEADS, HEAD_SIZE), jnp.bfloat16), key_vectors.reshape(PACKED_TOKENS, KEY_VALUE_HEADS, HEAD_SIZE)], axis=0)
    value_padded = jnp.concatenate([jnp.zeros((leading_rows, KEY_VALUE_HEADS, HEAD_SIZE), jnp.bfloat16), value_vectors.reshape(PACKED_TOKENS, KEY_VALUE_HEADS, HEAD_SIZE)], axis=0)
    doc_starts = jnp.cumsum(doc_lengths, dtype=jnp.int32) - doc_lengths
    local_pos = jnp.arange(CONTEXT_TOKENS, dtype=jnp.int32)
    complete_rows = WINDOW * CONTEXT_TOKENS

    def shard_step(grads, shard):
        first_pos = (shard * CONTEXT_TOKENS).astype(jnp.int32)
        query_pos = first_pos + local_pos
        query_doc = doc_index_of(query_pos, doc_starts)
        doc_start = jnp.max(jnp.where(doc_starts <= first_pos, doc_starts, 0))
        needed = jnp.clip(shard - doc_start // CONTEXT_TOKENS + 1, 1, WINDOW).astype(jnp.int32)
        block_q = lax.dynamic_index_in_dim(reshaped_query, shard, 0, keepdims=False)
        block_g = lax.dynamic_index_in_dim(reshaped_gradient, shard, 0, keepdims=False)

        def branch(slot_count):
            key_total_count = slot_count * CONTEXT_TOKENS
            begin = ((shard + WINDOW - slot_count) * CONTEXT_TOKENS).astype(jnp.int32)
            key_block = lax.dynamic_slice_in_dim(key_padded, begin, key_total_count, 0)
            value_block = lax.dynamic_slice_in_dim(value_padded, begin, key_total_count, 0)
            key_pos = first_pos + CONTEXT_TOKENS - key_total_count + jnp.arange(key_total_count, dtype=jnp.int32)
            key_doc = doc_index_of(key_pos, doc_starts)
            allowed = (query_doc[:, None] == key_doc[None, :]) & (key_pos[None, :] <= query_pos[:, None])
            output, grad_query, grad_key, grad_value = attend_all(block_q, block_g, key_block, value_block, allowed, score_scale)
            padded_width = jnp.zeros((complete_rows - key_total_count, KEY_VALUE_HEADS, HEAD_SIZE), jnp.float32)
            return (output, grad_query, jnp.concatenate([padded_width, grad_key], axis=0), jnp.concatenate([padded_width, grad_value], axis=0))
        output, grad_query, grad_key, grad_value = lax.switch(needed - 1, [partial(branch, count_slots) for count_slots in range(1, WINDOW + 1)])
        key_running_sum, value_running_sum = grads
        base_row = (shard * CONTEXT_TOKENS).astype(jnp.int32)
        key_running_sum = lax.dynamic_update_slice_in_dim(key_running_sum, lax.dynamic_slice_in_dim(key_running_sum, base_row, complete_rows, 0) + grad_key, base_row, 0)
        value_running_sum = lax.dynamic_update_slice_in_dim(value_running_sum, lax.dynamic_slice_in_dim(value_running_sum, base_row, complete_rows, 0) + grad_value, base_row, 0)
        return ((key_running_sum, value_running_sum), (output, grad_query))
    initial_state = (jnp.zeros((leading_rows + PACKED_TOKENS, KEY_VALUE_HEADS, HEAD_SIZE), jnp.float32), jnp.zeros((leading_rows + PACKED_TOKENS, KEY_VALUE_HEADS, HEAD_SIZE), jnp.float32))
    (key_running_sum, value_running_sum), (outputs, grad_qs) = lax.scan(shard_step, initial_state, jnp.arange(N_CTX, dtype=jnp.int32))
    attn_output = outputs.reshape(PACKED_TOKENS, QUERY_HEADS * HEAD_SIZE)
    grad_queries = grad_qs.reshape(PACKED_TOKENS, QUERY_HEADS * HEAD_SIZE)
    key_gradient = key_running_sum[leading_rows:].astype(jnp.bfloat16).reshape(PACKED_TOKENS, KEY_VALUE_HEADS * HEAD_SIZE)
    value_gradient = value_running_sum[leading_rows:].astype(jnp.bfloat16).reshape(PACKED_TOKENS, KEY_VALUE_HEADS * HEAD_SIZE)
    return (attn_output, grad_queries, key_gradient, value_gradient)
```

```python
import functools, math
import jax, jax.numpy as jnp
from jax import lax
from jax.sharding import PartitionSpec as P
from jax.experimental import pallas as pl
from jax.experimental.pallas import tpu as pltpu
D=128; T=256; W=8; H=8
SCALE=1.0/math.sqrt(D)
C2=SCALE*math.log2(math.e)
BIG=1e30
NT=(((1,),(1,)),((),()))
f32=jnp.float32; bf16=jnp.bfloat16

def doc_rows(lens_ref):
    sub=lax.broadcasted_iota(jnp.int32,(128,128),0); lane=lax.broadcasted_iota(jnp.int32,(128,128),1)
    lens=jnp.broadcast_to(lens_ref[...],(128,128))
    st=jnp.sum(jnp.where(lane<sub,lens,0.0),axis=1,keepdims=True)
    en=jnp.sum(jnp.where(lane<=sub,lens,0.0),axis=1,keepdims=True)
    st=jnp.transpose(jnp.broadcast_to(st,(128,128)))
    en=jnp.transpose(jnp.broadcast_to(en,(128,128)))
    last=lane==127
    st=jnp.where(last,-1e9,st); en=jnp.where(last,0.0,en)
    return st[0:1],en[0:1]

def attn_kernel(pos_ref,lens_ref,q_ref,g_ref,k_ref,v_ref,o_ref,dq_ref,dk_ref,dv_ref,
                kp,kT,vp,vT,qp,gp,s_ref,p_ref,dk_acc,dv_acc):
    first=pos_ref[0].astype(f32)
    lo,hi=doc_rows(lens_ref)
    sub=lax.broadcasted_iota(jnp.int32,(T,D),0).astype(f32)
    lane=lax.broadcasted_iota(jnp.int32,(T,D),1)
    qpos=first+sub
    qp[:,D:]=jnp.where((qpos>=lo)&(qpos<hi),0.0,-BIG).astype(bf16)
    three=jnp.where(lane<3,1.0,0.0).astype(bf16)
    for j in range(W):
        rows=slice(j*T,(j+1)*T)
        kpos=qpos-j*T
        kp[rows,:D]=k_ref[rows]
        kp[rows,D:]=jnp.where((kpos>=lo)&(kpos<hi),1.0,0.0).astype(bf16)
        vp[rows,:D]=v_ref[rows]
        vp[rows,D:]=three
        kT[:,rows]=jnp.transpose(k_ref[rows])
        vT[:D,rows]=jnp.transpose(v_ref[rows])
        vT[D:,rows]=jnp.ones((16,T),bf16)
    dk_acc[...]=jnp.zeros_like(dk_acc)
    dv_acc[...]=jnp.zeros_like(dv_acc)
    def head(h,_):
        col=pl.ds(pl.multiple_of(h*D,D),D)
        qh=q_ref[:,col]; gh=g_ref[:,col]
        qp[:,:D]=qh
        m=None
        for j in range(W):
            rows=slice(j*T,(j+1)*T)
            s=lax.dot_general(kp[rows],qp[...],NT,preferred_element_type=f32)
            if j==0:
                r=lax.broadcasted_iota(jnp.int32,(T,T),0); c=lax.broadcasted_iota(jnp.int32,(T,T),1)
                s=jnp.where(r<=c,s,-BIG)
            s_ref[rows]=s
            mj=jnp.max(s,axis=0,keepdims=True)
            m=mj if m is None else jnp.maximum(m,mj)
        mc=m*C2
        ot=None
        for j in range(W):
            rows=slice(j*T,(j+1)*T)
            pb=jnp.exp2(s_ref[rows]*C2-mc).astype(bf16)
            p_ref[rows]=pb
            x=jnp.dot(vT[:,rows],pb,preferred_element_type=f32)
            ot=x if ot is None else ot+x
        o=jnp.transpose(ot[:D])
        l=jnp.transpose(ot[D:D+8])[:,0:1]
        inv=1.0/l
        ob=(o*inv).astype(bf16)
        o_ref[:,col]=ob
        gf=gh.astype(f32)
        delta=jnp.sum(ob.astype(f32)*gf,axis=1,keepdims=True)
        rs=inv*SCALE
        g2=(gf*rs).astype(bf16)
        dl=-delta*rs
        d1=dl.astype(bf16).astype(f32); r1=dl-d1
        d2=r1.astype(bf16).astype(f32); d3=r1-d2
        gp[:,:D]=g2
        gp[:,D:]=jnp.where(lane==0,d1,jnp.where(lane==1,d2,jnp.where(lane==2,d3,0.0))).astype(bf16)
        dqt=None
        for j in range(W):
            rows=slice(j*T,(j+1)*T)
            dp=lax.dot_general(vp[rows],gp[...],NT,preferred_element_type=f32)
            pb=p_ref[rows]
            ds=(pb.astype(f32)*dp).astype(bf16)
            dv_acc[rows]+=jnp.dot(pb,g2,preferred_element_type=f32)
            dk_acc[rows]+=jnp.dot(ds,qh,preferred_element_type=f32)
            x=jnp.dot(kT[:,rows],ds,preferred_element_type=f32)
            dqt=x if dqt is None else dqt+x
        dq_ref[:,col]=jnp.transpose(dqt).astype(bf16)
        return 0
    lax.fori_loop(0,H,head,0)
    dk_ref[...]=dk_acc[...].astype(bf16)
    dv_ref[...]=(dv_acc[...]*(1.0/SCALE)).astype(bf16)

def attn(pos,lens,q,g,k,v):
    vm=pl.BlockSpec(memory_space=pltpu.VMEM)
    return pl.pallas_call(attn_kernel,
        out_shape=(jax.ShapeDtypeStruct((T,H*D),bf16),jax.ShapeDtypeStruct((T,H*D),bf16),
                   jax.ShapeDtypeStruct((W*T,D),bf16),jax.ShapeDtypeStruct((W*T,D),bf16)),
        in_specs=[pl.BlockSpec(memory_space=pltpu.SMEM)]+[vm]*5, out_specs=(vm,)*4,
        scratch_shapes=[pltpu.VMEM((W*T,2*D),bf16),pltpu.VMEM((D,W*T),bf16),pltpu.VMEM((W*T,2*D),bf16),pltpu.VMEM((D+16,W*T),bf16),
                        pltpu.VMEM((T,2*D),bf16),pltpu.VMEM((T,2*D),bf16),pltpu.VMEM((W*T,T),f32),pltpu.VMEM((W*T,T),bf16),
                        pltpu.VMEM((W*T,D),f32),pltpu.VMEM((W*T,D),f32)],
        name="attn")(pos,lens,q,g,k,v)


WINDOW = 8


def shifted(value, axis, steps):
    count = lax.axis_size(axis)
    leading, last = (max(0, -steps), min(count, count - steps))
    return lax.ppermute(value, axis, [(source, source + steps) for source in range(leading, last)])


def body(queries, key_vectors, value_vectors, output_gradient, doc_lengths):
    ctx_index = lax.axis_index("ctx")
    k_heads, v_heads = (
        lax.all_to_all(key_vectors, "tp", split_axis=1, concat_axis=0, tiled=True),
        lax.all_to_all(value_vectors, "tp", split_axis=1, concat_axis=0, tiled=True),
    )
    kv_local = jnp.concatenate([k_heads, v_heads], axis=1)
    slots = [kv_local] + [shifted(kv_local, "ctx", j) for j in range(1, WINDOW)]
    window = jnp.concatenate(slots, axis=0)
    lens = jnp.pad(doc_lengths.astype(f32).reshape(1, -1), ((0, 0), (0, 128 - doc_lengths.shape[0])))
    pos = (ctx_index * T).astype(jnp.int32).reshape(1)
    out, dq, dk, dv = attn(pos, lens, queries, output_gradient, window[:, :D], window[:, D:])
    grads = jnp.concatenate([dk, dv], axis=1).reshape(WINDOW, T, 2 * D)
    own = grads[0].astype(f32)
    for j in range(1, WINDOW):
        own = own + shifted(grads[j], "ctx", -j).astype(f32)
    own = own.astype(bf16)
    dkg = lax.all_to_all(own[:, :D], "tp", split_axis=0, concat_axis=1, tiled=True)
    dvg = lax.all_to_all(own[:, D:], "tp", split_axis=0, concat_axis=1, tiled=True)
    return out, dq, dkg, dvg


def solution(mesh):
    return jax.shard_map(
        body,
        mesh=mesh,
        in_specs=(P("ctx", "tp"), P(("ctx", "tp"), None), P(("ctx", "tp"), None), P("ctx", "tp"), P()),
        out_specs=(P("ctx", "tp"), P("ctx", "tp"), P(("ctx", "tp"), None), P(("ctx", "tp"), None)),
        check_vma=False,
    )
```

```python
import functools
import math

import jax
import jax.numpy as jnp
from jax import lax
from jax.experimental import pallas as pl
from jax.experimental.pallas import tpu as pltpu
from jax.sharding import PartitionSpec as P

D = 128
T = 256
W = 8
H = 8
NX = 4
ND = 8
ROWS = T // ND
SCALE = 1.0 / math.sqrt(D)
C2 = SCALE * math.log2(math.e)
BIG = 1e30
NT = (((1,), (1,)), ((), ()))
f32 = jnp.float32
bf16 = jnp.bfloat16
MESH = pl.DeviceIdType.MESH


ORDER = (7, 5, 6, 3, 4, 1, 2, 0)
KEYS = slice(0, T)
VALUES = slice(T, 2 * T)


def doc_rows(lens_ref):
    n = lens_ref.shape[1]
    sub = lax.broadcasted_iota(jnp.int32, (128, n), 0)
    lane = lax.broadcasted_iota(jnp.int32, (128, n), 1)
    lens = jnp.broadcast_to(lens_ref[...].astype(f32), (128, n))
    st = jnp.sum(jnp.where(lane < sub, lens, 0.0), axis=1, keepdims=True)
    en = jnp.sum(jnp.where(lane <= sub, lens, 0.0), axis=1, keepdims=True)
    st = jnp.transpose(jnp.broadcast_to(st, (128, 128)))
    en = jnp.transpose(jnp.broadcast_to(en, (128, 128)))
    last = lax.broadcasted_iota(jnp.int32, (128, 128), 1) == 127
    st = jnp.where(last, -1e9, st)
    en = jnp.where(last, 0.0, en)
    return st[0:1], en[0:1]


def kernel(
    nctx, lens_ref, q_hbm, g_hbm, k_hbm, v_hbm, o_ref, dq_ref, dk_ref, dv_ref,
    q_ref, g_ref, kv, gb, pst, xst, zst, fin, kg, vg,
    qa, kb, three, qall, g2all, dall, kT, vT, m_ref, s_ref, p_ref, ds_ref,
    lsem, asend, arecv, zsend, zrecv, xsend, xrecv, psend, precv,
):
    i = lax.axis_index("ctx")
    me = lax.axis_index("tp")
    core = lax.rem(i, 2)
    x = lax.rem(lax.div(i, 2), NX)
    row = i - lax.rem(i, 2 * NX)
    base = lax.rem(i, 2 * NX)
    partner = i + 1 - 2 * core
    up = lax.rem(i + 2 * NX, nctx)
    down = lax.rem(i + nctx - 2 * NX, nctx)

    def chip(j):
        return row + lax.rem(base + 2 * j, 2 * NX)

    def peer(d):
        return lax.rem(me + d, ND)

    def remote(src, dst, send, recv, who):
        return pltpu.make_async_remote_copy(
            src_ref=src, dst_ref=dst, send_sem=send, recv_sem=recv, device_id=who, device_id_type=MESH
        )

    own_col = pl.ds(pl.multiple_of(me * D, D), D)
    own_row = [pl.ds(pl.multiple_of(half * T + me * ROWS, ROWS), ROWS) for half in (0, 1)]
    source = (k_hbm, v_hbm)
    loads = [pltpu.make_async_copy(q_hbm, q_ref, lsem.at[0]), pltpu.make_async_copy(g_hbm, g_ref, lsem.at[1])]
    for half in (0, 1):
        loads.append(
            pltpu.make_async_copy(source[half].at[:, own_col], kv.at[0, own_row[half]], lsem.at[2 + half])
        )
    for copy in loads:
        copy.start()

    barrier = pltpu.get_barrier_semaphore()
    greeted = [(i, peer(d)) for d in range(1, ND)]
    greeted += [(c, me) for c in (partner, up, down, chip(1), chip(2), chip(3))]
    for who in greeted:
        pl.semaphore_signal(barrier, inc=1, device_id=who, device_id_type=MESH)
    pl.semaphore_wait(barrier, len(greeted))

    spread = [[], []]
    for half in (0, 1):
        for d in range(1, ND):
            col = pl.ds(pl.multiple_of(peer(d) * D, D), D)
            copy = remote(
                source[half].at[:, col], kv.at[0, own_row[half]], asend.at[half, d], arecv.at[half, d], (i, peer(d))
            )
            copy.start()
            spread[half].append(copy)

    lo, hi = doc_rows(lens_ref)
    pos0 = (i * T).astype(f32)
    sub = lax.broadcasted_iota(jnp.int32, (T, D), 0).astype(f32)
    lane = lax.broadcasted_iota(jnp.int32, (T, D), 1)
    qpos = pos0 + sub
    qa[...] = jnp.where((qpos >= lo) & (qpos < hi), 0.0, -BIG).astype(bf16)
    three[...] = jnp.where(lane < 3, 1.0, 0.0).astype(bf16)
    for j in range(W):
        kpos = qpos - j * T
        kb[j * T : (j + 1) * T] = jnp.where((kpos >= lo) & (kpos < hi), 1.0, 0.0).astype(bf16)
    vT[D:] = jnp.ones((16, W * T), bf16)
    m_ref[...] = jnp.full(m_ref.shape, -3e38, f32)
    loads[0].wait()
    loads[1].wait()
    for h in range(H):
        qall[h * T : (h + 1) * T] = q_ref[:, h * D : (h + 1) * D]

    half_of = (KEYS, VALUES)

    def zcopy(half):
        part = half_of[half]
        return remote(kv.at[0, part], kv.at[8, part], zsend.at[half], zrecv.at[half], (up, me))

    def xcopy(j, half):
        part = half_of[half]
        src = jnp.where(x + j < NX, 0, 8)
        return remote(kv.at[src, part], kv.at[2 * j, part], xsend.at[half, j], xrecv.at[half, j], (chip(j), me))

    def share(m, half):
        part = half_of[half]
        return remote(
            kv.at[2 * (m + core), part], kv.at[2 * m + 1, part], psend.at[half, m], precv.at[half, m], (partner, me)
        )

    for half in (0, 1):
        loads[2 + half].wait()
        for copy in spread[half]:
            copy.wait()
        zcopy(half).start()
        for j in (1, 3, 2):
            pl.when(x + j < NX)(xcopy(j, half).start)
        pl.when(core == 0)(lambda half=half: share(0, half).start())

    def scores(j):
        rows = slice(j * T, (j + 1) * T)
        keys = kv[j, KEYS]
        kT[:, rows] = jnp.transpose(keys)
        left = jnp.concatenate([keys, kb[rows]], axis=1)
        for h in range(H):
            cols = slice(h * T, (h + 1) * T)
            right = jnp.concatenate([qall[cols], qa[...]], axis=1)
            s = lax.dot_general(left, right, NT, preferred_element_type=f32)
            if j == 0:
                r = lax.broadcasted_iota(jnp.int32, (T, T), 0)
                c = lax.broadcasted_iota(jnp.int32, (T, T), 1)
                s = jnp.where(r <= c, s, -BIG)
            s_ref[rows, cols] = s
            m_ref[:, cols] = jnp.maximum(m_ref[:, cols], jnp.max(s.reshape(T // 8, 8, T), axis=0))

    scores(0)
    for half in (0, 1):
        zcopy(half).wait_recv()
        for j in (1, 3, 2):
            pl.when(x + j >= NX)(xcopy(j, half).start)
        pl.when(core == 1)(lambda half=half: share(3, half).start())
    for j in (1, 3, 2):
        xcopy(j, 0).wait_recv()
        share(j - core, 0).start()
        scores(2 * j)
    for j in (1, 3, 2):
        xcopy(j, 1).wait_recv()
        share(j - core, 1).start()
    for m in range(4):
        share(m, 0).wait()
        scores(2 * m + 1)
    for m in range(4):
        share(m, 1).wait()
    for half in (0, 1):
        zcopy(half).wait_send()
        for j in (1, 3, 2):
            xcopy(j, half).wait_send()
    for j in range(W):
        vT[:D, j * T : (j + 1) * T] = jnp.transpose(kv[j, VALUES])

    for h in range(H):
        cols = slice(h * T, (h + 1) * T)
        col = slice(h * D, (h + 1) * D)
        mc = jnp.max(m_ref[:, cols], axis=0, keepdims=True) * C2
        for j in range(W):
            rows = slice(j * T, (j + 1) * T)
            p_ref[rows, cols] = jnp.exp2(s_ref[rows, cols] * C2 - mc).astype(bf16)
        ot = jnp.dot(vT[...], p_ref[:, cols], preferred_element_type=f32)
        o = jnp.transpose(ot[:D])
        total = jnp.transpose(ot[D : D + 8])[:, 0:1]
        inv = 1.0 / total
        ob = (o * inv).astype(bf16)
        o_ref[:, col] = ob
        gf = g_ref[:, col].astype(f32)
        delta = jnp.sum(ob.astype(f32) * gf, axis=1, keepdims=True)
        rs = inv * SCALE
        g2all[cols] = (gf * rs).astype(bf16)
        dl = -delta * rs
        d1 = dl.astype(bf16).astype(f32)
        r1 = dl - d1
        d2 = r1.astype(bf16).astype(f32)
        d3 = r1 - d2
        dall[cols] = jnp.where(lane == 0, d1, jnp.where(lane == 1, d2, jnp.where(lane == 2, d3, 0.0))).astype(bf16)

    def gradients(j):
        rows = slice(j * T, (j + 1) * T)
        left = jnp.concatenate([kv[j, VALUES], three[...]], axis=1)
        dv = jnp.dot(p_ref[rows], g2all[...], preferred_element_type=f32)
        dk = None
        for part in range(2):
            for h in range(part * H // 2, (part + 1) * H // 2):
                cols = slice(h * T, (h + 1) * T)
                right = jnp.concatenate([g2all[cols], dall[cols]], axis=1)
                dp = lax.dot_general(left, right, NT, preferred_element_type=f32)
                ds_ref[rows, cols] = (p_ref[rows, cols].astype(f32) * dp).astype(bf16)
            cols = slice(part * H // 2 * T, (part + 1) * H // 2 * T)
            piece = jnp.dot(ds_ref[rows, cols], qall[cols], preferred_element_type=f32)
            dk = piece if dk is None else dk + piece
        return dk, dv * (1.0 / SCALE)

    def query_gradient(h):
        cols = slice(h * T, (h + 1) * T)
        dqt = jnp.dot(kT[...], ds_ref[:, cols], preferred_element_type=f32)
        dq_ref[:, h * D : (h + 1) * D] = jnp.transpose(dqt).astype(bf16)

    def give(m):
        return remote(gb.at[2 * m + 1], pst.at[m], psend.at[2, m], precv.at[2, m], (partner, me))

    def xback(j, half):
        part = half_of[half]
        return remote(
            gb.at[2 * j, part], xst.at[j, part], xsend.at[2 + half, j], xrecv.at[2 + half, j], (chip(NX - j), me)
        )

    def zback(half):
        part = half_of[half]
        return remote(gb.at[8, part], zst.at[part], zsend.at[2 + half], zrecv.at[2 + half], (down, me))

    own = None
    for j in ORDER:
        dk, dv = gradients(j)
        if j == 0:
            own = [dk, dv]
        elif j % 2:
            gb[j, KEYS] = dk.astype(bf16)
            gb[j, VALUES] = dv.astype(bf16)
            give(j // 2).start()
        else:
            if j == 6:
                give(3).wait()
                give(2).wait()
            elif j == 4:
                give(1).wait()
            else:
                give(0).wait()
            other = pst[j // 2 - core].astype(f32)
            gb[j, KEYS] = (dk + other[:T]).astype(bf16)
            gb[j, VALUES] = (dv + other[T:]).astype(bf16)
            for half in (0, 1):
                xback(j // 2, half).start()

    first_part = jnp.where(core == 0, 1.0, 0.0)
    last_part = jnp.where(core == 1, 1.0, 0.0)
    for h in range(3):
        query_gradient(h)
    prev = [None, None]
    for half in (0, 1):
        part = half_of[half]
        own[half] += pst[0, part].astype(f32) * first_part
        prev[half] = pst[3, part].astype(f32) * last_part
        for j in (3, 2, 1):
            xback(j, half).wait()
            mine = jnp.where(x + j < NX, 1.0, 0.0)
            got = xst[j, part].astype(f32)
            own[half] += got * mine
            prev[half] += got * (1.0 - mine)
        gb[8, part] = prev[half].astype(bf16)
        zback(half).start()
    for h in range(3, 6):
        query_gradient(h)
    out = (kg, vg)
    last = []
    for half in (0, 1):
        part = half_of[half]
        zback(half).wait()
        fin[part] = (own[half] + zst[part].astype(f32)).astype(bf16)
        for d in range(1, ND):
            rows = pl.ds(pl.multiple_of(half * T + peer(d) * ROWS, ROWS), ROWS)
            copy = remote(
                fin.at[rows], out[half].at[:, own_col], asend.at[2 + half, d], arecv.at[2 + half, d], (i, peer(d))
            )
            copy.start()
            last.append(copy)
    for h in range(6, 8):
        query_gradient(h)
    kg[:, own_col] = fin[own_row[0]]
    vg[:, own_col] = fin[own_row[1]]
    for copy in last:
        copy.wait()
    dk_ref[...] = kg[...]
    dv_ref[...] = vg[...]


def write_kernel(o_in, dq_in, dk_in, dv_in, o_out, dq_out, dk_out, dv_out, sem):
    pairs = ((o_in, o_out), (dq_in, dq_out), (dk_in, dk_out), (dv_in, dv_out))
    copies = [pltpu.make_async_copy(a, b, sem.at[n]) for n, (a, b) in enumerate(pairs)]
    for copy in copies:
        copy.start()
    for copy in copies:
        copy.wait()


def body(queries, key_vectors, value_vectors, output_gradient, doc_lengths):
    vm = pl.BlockSpec(memory_space=pltpu.VMEM)
    free = pl.BlockSpec(memory_space=pl.ANY)
    dma = pltpu.SemaphoreType.DMA
    vmem = pltpu.VMEM
    big = jax.ShapeDtypeStruct((T, H * D), bf16)
    small = jax.ShapeDtypeStruct((ROWS, ND * D), bf16)
    arrays = [
        pltpu.with_memory_space_constraint(a, pltpu.HBM)
        for a in (queries, output_gradient, key_vectors, value_vectors)
    ]
    parts = pl.pallas_call(
        functools.partial(kernel, lax.axis_size("ctx")),
        out_shape=(big, big, small, small),
        in_specs=[vm] + [free] * 4,
        out_specs=(vm,) * 4,
        scratch_shapes=[
            vmem((T, H * D), bf16),
            vmem((T, H * D), bf16),
            vmem((9, 2 * T, D), bf16),
            vmem((9, 2 * T, D), bf16),
            vmem((4, 2 * T, D), bf16),
            vmem((4, 2 * T, D), bf16),
            vmem((2 * T, D), bf16),
            vmem((2 * T, D), bf16),
            vmem((ROWS, ND * D), bf16),
            vmem((ROWS, ND * D), bf16),
            vmem((T, D), bf16),
            vmem((W * T, D), bf16),
            vmem((T, D), bf16),
            vmem((H * T, D), bf16),
            vmem((H * T, D), bf16),
            vmem((H * T, D), bf16),
            vmem((D, W * T), bf16),
            vmem((D + 16, W * T), bf16),
            vmem((8, H * T), f32),
            vmem((W * T, H * T), f32),
            vmem((W * T, H * T), bf16),
            vmem((W * T, H * T), bf16),
            dma((4,)),
            dma((4, ND)),
            dma((4, ND)),
            dma((4,)),
            dma((4,)),
            dma((4, NX)),
            dma((4, NX)),
            dma((3, 4)),
            dma((3, 4)),
        ],
        compiler_params=pltpu.CompilerParams(
            collective_id=0, has_side_effects=True, vmem_limit_bytes=52 << 20
        ),
        name="attention",
    )(doc_lengths.reshape(1, -1), *arrays)
    return pl.pallas_call(
        write_kernel,
        out_shape=(big, big, small, small),
        in_specs=[free] * 4,
        out_specs=(free,) * 4,
        scratch_shapes=[dma((4,))],
        compiler_params=pltpu.CompilerParams(vmem_limit_bytes=2 << 20),
        name="write",
    )(*parts)


def solution(mesh):
    return jax.shard_map(
        body,
        mesh=mesh,
        in_specs=(P("ctx", "tp"), P(("ctx", "tp"), None), P(("ctx", "tp"), None), P("ctx", "tp"), P()),
        out_specs=(P("ctx", "tp"), P("ctx", "tp"), P(("ctx", "tp"), None), P(("ctx", "tp"), None)),
        check_vma=False,
    )
```

```python
import functools
import math

import jax
import jax.numpy as jnp
from jax import lax
from jax.experimental import pallas as pl
from jax.experimental.pallas import tpu as pltpu
from jax.sharding import PartitionSpec as P

D = 128
T = 256
W = 8
H = 8
NX = 4
ND = 8
ROWS = T // ND
SCALE = 1.0 / math.sqrt(D)
C2 = SCALE * math.log2(math.e)
BIG = 1e30
NT = (((1,), (1,)), ((), ()))
f32 = jnp.float32
bf16 = jnp.bfloat16
MESH = pl.DeviceIdType.MESH


KEYS = slice(0, T)
VALUES = slice(T, 2 * T)


def doc_rows(lens_ref):
    n = lens_ref.shape[1]
    sub = lax.broadcasted_iota(jnp.int32, (128, n), 0)
    lane = lax.broadcasted_iota(jnp.int32, (128, n), 1)
    lens = jnp.broadcast_to(lens_ref[...].astype(f32), (128, n))
    st = jnp.sum(jnp.where(lane < sub, lens, 0.0), axis=1, keepdims=True)
    en = jnp.sum(jnp.where(lane <= sub, lens, 0.0), axis=1, keepdims=True)
    st = jnp.transpose(jnp.broadcast_to(st, (128, 128)))
    en = jnp.transpose(jnp.broadcast_to(en, (128, 128)))
    last = lax.broadcasted_iota(jnp.int32, (128, 128), 1) == 127
    st = jnp.where(last, -1e9, st)
    en = jnp.where(last, 0.0, en)
    return st[0:1], en[0:1]


def kernel(
    nctx, lens_ref, q_hbm, g_hbm, k_hbm, v_hbm, o_ref, dq_ref, dk_ref, dv_ref,
    q_ref, g_ref, kv, gb, pst, xst, zst, own, fin, kg, vg,
    qa, kb, three, qall, g2all, dall, kT, vT, m_ref, s_ref, p_ref, ds_ref,
    lsem, asend, arecv, zsend, zrecv, xsend, xrecv, psend, precv,
):
    i = lax.axis_index("ctx")
    me = lax.axis_index("tp")
    core = lax.rem(i, 2)
    x = lax.rem(lax.div(i, 2), NX)
    row = i - lax.rem(i, 2 * NX)
    base = lax.rem(i, 2 * NX)
    partner = i + 1 - 2 * core
    up = lax.rem(i + 2 * NX, nctx)
    down = lax.rem(i + nctx - 2 * NX, nctx)
    z = lax.div(i, 2 * NX)
    not_first = z > 0
    not_last = z < nctx // (2 * NX) - 1

    def chip(j):
        return row + lax.rem(base + 2 * j, 2 * NX)

    def peer(d):
        return lax.rem(me + d, ND)

    def remote(src, dst, send, recv, who):
        return pltpu.make_async_remote_copy(
            src_ref=src, dst_ref=dst, send_sem=send, recv_sem=recv, device_id=who, device_id_type=MESH
        )

    own_col = pl.ds(pl.multiple_of(me * D, D), D)
    own_row = [pl.ds(pl.multiple_of(half * T + me * ROWS, ROWS), ROWS) for half in (0, 1)]
    source = (k_hbm, v_hbm)
    loads = [pltpu.make_async_copy(q_hbm, q_ref, lsem.at[0]), pltpu.make_async_copy(g_hbm, g_ref, lsem.at[1])]
    for half in (0, 1):
        loads.append(
            pltpu.make_async_copy(source[half].at[:, own_col], kv.at[0, own_row[half]], lsem.at[2 + half])
        )
    for copy in loads:
        copy.start()

    barrier = pltpu.get_barrier_semaphore()
    greeted = [(i, peer(d)) for d in range(1, ND)]
    greeted += [(c, me) for c in (partner, chip(1), chip(2), chip(3))]
    for who in greeted:
        pl.semaphore_signal(barrier, inc=1, device_id=who, device_id_type=MESH)
    pl.when(not_first)(
        lambda: pl.semaphore_signal(barrier, inc=1, device_id=(down, me), device_id_type=MESH)
    )
    pl.semaphore_wait(barrier, len(greeted) + jnp.where(not_last, 1, 0))

    spread = [[], []]
    for half in (0, 1):
        for d in range(1, ND):
            col = pl.ds(pl.multiple_of(peer(d) * D, D), D)
            copy = remote(
                source[half].at[:, col], kv.at[0, own_row[half]], asend.at[half, d], arecv.at[half, d], (i, peer(d))
            )
            copy.start()
            spread[half].append(copy)

    @pl.when(jnp.logical_not(not_first))
    def _():
        kv[8] = jnp.zeros((2 * T, D), bf16)

    @pl.when(jnp.logical_not(not_last))
    def _():
        zst[...] = jnp.zeros(zst.shape, bf16)

    lo, hi = doc_rows(lens_ref)
    pos0 = (i * T).astype(f32)
    sub = lax.broadcasted_iota(jnp.int32, (T, D), 0).astype(f32)
    lane = lax.broadcasted_iota(jnp.int32, (T, D), 1)
    qpos = pos0 + sub
    qa[...] = jnp.where((qpos >= lo) & (qpos < hi), 0.0, -BIG).astype(bf16)
    three[...] = jnp.where(lane < 3, 1.0, 0.0).astype(bf16)
    for j in range(W):
        kpos = qpos - j * T
        kb[j * T : (j + 1) * T] = jnp.where((kpos >= lo) & (kpos < hi), 1.0, 0.0).astype(bf16)
    vT[D:] = jnp.ones((16, W * T), bf16)
    m_ref[...] = jnp.full(m_ref.shape, -3e38, f32)
    loads[0].wait()
    loads[1].wait()
    for h in range(H):
        qall[h * T : (h + 1) * T] = q_ref[:, h * D : (h + 1) * D]

    half_of = (KEYS, VALUES)

    def zcopy(half):
        part = half_of[half]
        return remote(kv.at[0, part], kv.at[8, part], zsend.at[half], zrecv.at[half], (up, me))

    def xcopy(j, half):
        part = half_of[half]
        src = jnp.where(x + j < NX, 0, 8)
        return remote(kv.at[src, part], kv.at[2 * j, part], xsend.at[half, j], xrecv.at[half, j], (chip(j), me))

    def share(m, half):
        part = half_of[half]
        return remote(
            kv.at[2 * (m + core), part], kv.at[2 * m + 1, part], psend.at[half, m], precv.at[half, m], (partner, me)
        )

    for half in (0, 1):
        loads[2 + half].wait()
        for copy in spread[half]:
            copy.wait()
        pl.when(not_last)(zcopy(half).start)
        for j in (1, 3, 2):
            pl.when(x + j < NX)(xcopy(j, half).start)
        pl.when(core == 0)(lambda half=half: share(0, half).start())

    def scores(j):
        rows = slice(j * T, (j + 1) * T)
        keys = kv[j, KEYS]
        kT[:, rows] = jnp.transpose(keys)
        left = jnp.concatenate([keys, kb[rows]], axis=1)
        for h in range(H):
            cols = slice(h * T, (h + 1) * T)
            right = jnp.concatenate([qall[cols], qa[...]], axis=1)
            s = lax.dot_general(left, right, NT, preferred_element_type=f32)
            if j == 0:
                r = lax.broadcasted_iota(jnp.int32, (T, T), 0)
                c = lax.broadcasted_iota(jnp.int32, (T, T), 1)
                s = jnp.where(r <= c, s, -BIG)
            s_ref[rows, cols] = s
            m_ref[:, cols] = jnp.maximum(m_ref[:, cols], jnp.max(s.reshape(T // 8, 8, T), axis=0))

    scores(0)
    for half in (0, 1):
        pl.when(not_first)(zcopy(half).wait_recv)
        for j in (1, 3, 2):
            pl.when(x + j >= NX)(xcopy(j, half).start)
        pl.when(core == 1)(lambda half=half: share(3, half).start())
    for j in (1, 3, 2):
        xcopy(j, 0).wait_recv()
        share(j - core, 0).start()
        scores(2 * j)
    for j in (1, 3, 2):
        xcopy(j, 1).wait_recv()
        share(j - core, 1).start()
    for m in range(4):
        share(m, 0).wait()
        scores(2 * m + 1)
    for m in range(4):
        share(m, 1).wait()
    for half in (0, 1):
        pl.when(not_last)(zcopy(half).wait_send)
        for j in (1, 3, 2):
            xcopy(j, half).wait_send()
    for j in range(W):
        vT[:D, j * T : (j + 1) * T] = jnp.transpose(kv[j, VALUES])

    for h in range(H):
        cols = slice(h * T, (h + 1) * T)
        col = slice(h * D, (h + 1) * D)
        mc = jnp.max(m_ref[:, cols], axis=0, keepdims=True) * C2
        for j in range(W):
            rows = slice(j * T, (j + 1) * T)
            p_ref[rows, cols] = jnp.exp2(s_ref[rows, cols] * C2 - mc).astype(bf16)
        ot = jnp.dot(vT[...], p_ref[:, cols], preferred_element_type=f32)
        o = jnp.transpose(ot[:D])
        total = jnp.transpose(ot[D : D + 8])[:, 0:1]
        inv = 1.0 / total
        ob = (o * inv).astype(bf16)
        o_ref[:, col] = ob
        gf = g_ref[:, col].astype(f32)
        delta = jnp.sum(ob.astype(f32) * gf, axis=1, keepdims=True)
        rs = inv * SCALE
        g2all[cols] = (gf * rs).astype(bf16)
        dl = -delta * rs
        d1 = dl.astype(bf16).astype(f32)
        r1 = dl - d1
        d2 = r1.astype(bf16).astype(f32)
        d3 = r1 - d2
        dall[cols] = jnp.where(lane == 0, d1, jnp.where(lane == 1, d2, jnp.where(lane == 2, d3, 0.0))).astype(bf16)

    def value_gradient(j):
        rows = slice(j * T, (j + 1) * T)
        return jnp.dot(p_ref[rows], g2all[...], preferred_element_type=f32) * (1.0 / SCALE)

    def key_gradient(j):
        rows = slice(j * T, (j + 1) * T)
        left = jnp.concatenate([kv[j, VALUES], three[...]], axis=1)
        dk = None
        for part in range(2):
            for h in range(part * H // 2, (part + 1) * H // 2):
                cols = slice(h * T, (h + 1) * T)
                right = jnp.concatenate([g2all[cols], dall[cols]], axis=1)
                dp = lax.dot_general(left, right, NT, preferred_element_type=f32)
                ds_ref[rows, cols] = (p_ref[rows, cols].astype(f32) * dp).astype(bf16)
            cols = slice(part * H // 2 * T, (part + 1) * H // 2 * T)
            piece = jnp.dot(ds_ref[rows, cols], qall[cols], preferred_element_type=f32)
            dk = piece if dk is None else dk + piece
        return dk

    gradient = (key_gradient, value_gradient)

    def query_gradient(h):
        cols = slice(h * T, (h + 1) * T)
        dqt = jnp.dot(kT[...], ds_ref[:, cols], preferred_element_type=f32)
        dq_ref[:, h * D : (h + 1) * D] = jnp.transpose(dqt).astype(bf16)

    def give(m, half):
        part = half_of[half]
        return remote(
            gb.at[2 * m + 1, part], pst.at[m, part], psend.at[2 + half, m], precv.at[2 + half, m], (partner, me)
        )

    def xback(j, half):
        part = half_of[half]
        return remote(
            gb.at[2 * j, part], xst.at[j, part], xsend.at[2 + half, j], xrecv.at[2 + half, j], (chip(NX - j), me)
        )

    def zback(half):
        part = half_of[half]
        return remote(gb.at[8, part], zst.at[part], zsend.at[2 + half], zrecv.at[2 + half], (down, me))

    def odd(j, half):
        gb[j, half_of[half]] = gradient[half](j).astype(bf16)
        give(j // 2, half).start()

    def even(j, half):
        part = half_of[half]
        grad = gradient[half](j)
        for m in {6: (3, 2), 4: (1,), 2: (0,)}[j]:
            give(m, half).wait()
        gb[j, part] = (grad + pst[j // 2 - core, part].astype(f32)).astype(bf16)
        xback(j // 2, half).start()

    first_part = jnp.where(core == 0, 1.0, 0.0)
    last_part = jnp.where(core == 1, 1.0, 0.0)

    def fold(half):
        part = half_of[half]
        total = own[part] + pst[0, part].astype(f32) * first_part
        prev = pst[3, part].astype(f32) * last_part
        for j in (3, 2, 1):
            xback(j, half).wait()
            mine = jnp.where(x + j < NX, 1.0, 0.0)
            got = xst[j, part].astype(f32)
            total += got * mine
            prev += got * (1.0 - mine)
        gb[8, part] = prev.astype(bf16)
        pl.when(not_first)(zback(half).start)
        own[part] = total

    out = (kg, vg)
    last = []

    def finish(half):
        part = half_of[half]
        pl.when(not_last)(zback(half).wait_recv)
        fin[part] = (own[part] + zst[part].astype(f32)).astype(bf16)
        for d in range(1, ND):
            rows = pl.ds(pl.multiple_of(half * T + peer(d) * ROWS, ROWS), ROWS)
            copy = remote(
                fin.at[rows], out[half].at[:, own_col], asend.at[2 + half, d], arecv.at[2 + half, d], (i, peer(d))
            )
            copy.start()
            last.append(copy)

    for j in (7, 5, 3, 1):
        odd(j, 1)
    for j in (6, 4, 2):
        even(j, 1)
    own[VALUES] = value_gradient(0)
    for j in (7, 5, 3, 1):
        odd(j, 0)
    even(6, 0)
    fold(1)
    for j in (4, 2):
        even(j, 0)
    own[KEYS] = key_gradient(0)
    for h in range(4):
        query_gradient(h)
    finish(1)
    for h in range(4, 6):
        query_gradient(h)
    fold(0)
    for h in range(6, 8):
        query_gradient(h)
    finish(0)
    kg[:, own_col] = fin[own_row[0]]
    vg[:, own_col] = fin[own_row[1]]
    for half in (0, 1):
        pl.when(not_first)(zback(half).wait_send)
    for copy in last:
        copy.wait()
    dk_ref[...] = kg[...]
    dv_ref[...] = vg[...]


def write_kernel(o_in, dq_in, dk_in, dv_in, o_out, dq_out, dk_out, dv_out, sem):
    pairs = ((o_in, o_out), (dq_in, dq_out), (dk_in, dk_out), (dv_in, dv_out))
    copies = [pltpu.make_async_copy(a, b, sem.at[n]) for n, (a, b) in enumerate(pairs)]
    for copy in copies:
        copy.start()
    for copy in copies:
        copy.wait()


def body(queries, key_vectors, value_vectors, output_gradient, doc_lengths):
    vm = pl.BlockSpec(memory_space=pltpu.VMEM)
    free = pl.BlockSpec(memory_space=pl.ANY)
    dma = pltpu.SemaphoreType.DMA
    vmem = pltpu.VMEM
    big = jax.ShapeDtypeStruct((T, H * D), bf16)
    small = jax.ShapeDtypeStruct((ROWS, ND * D), bf16)
    arrays = [
        pltpu.with_memory_space_constraint(a, pltpu.HBM)
        for a in (queries, output_gradient, key_vectors, value_vectors)
    ]
    parts = pl.pallas_call(
        functools.partial(kernel, lax.axis_size("ctx")),
        out_shape=(big, big, small, small),
        in_specs=[vm] + [free] * 4,
        out_specs=(vm,) * 4,
        scratch_shapes=[
            vmem((T, H * D), bf16),
            vmem((T, H * D), bf16),
            vmem((9, 2 * T, D), bf16),
            vmem((9, 2 * T, D), bf16),
            vmem((4, 2 * T, D), bf16),
            vmem((4, 2 * T, D), bf16),
            vmem((2 * T, D), bf16),
            vmem((2 * T, D), f32),
            vmem((2 * T, D), bf16),
            vmem((ROWS, ND * D), bf16),
            vmem((ROWS, ND * D), bf16),
            vmem((T, D), bf16),
            vmem((W * T, D), bf16),
            vmem((T, D), bf16),
            vmem((H * T, D), bf16),
            vmem((H * T, D), bf16),
            vmem((H * T, D), bf16),
            vmem((D, W * T), bf16),
            vmem((D + 16, W * T), bf16),
            vmem((8, H * T), f32),
            vmem((W * T, H * T), f32),
            vmem((W * T, H * T), bf16),
            vmem((W * T, H * T), bf16),
            dma((4,)),
            dma((4, ND)),
            dma((4, ND)),
            dma((4,)),
            dma((4,)),
            dma((4, NX)),
            dma((4, NX)),
            dma((4, 4)),
            dma((4, 4)),
        ],
        compiler_params=pltpu.CompilerParams(
            collective_id=0, has_side_effects=True, vmem_limit_bytes=52 << 20
        ),
        name="attention",
    )(doc_lengths.reshape(1, -1), *arrays)
    return pl.pallas_call(
        write_kernel,
        out_shape=(big, big, small, small),
        in_specs=[free] * 4,
        out_specs=(free,) * 4,
        scratch_shapes=[dma((4,))],
        compiler_params=pltpu.CompilerParams(vmem_limit_bytes=2 << 20),
        name="write",
    )(*parts)


def solution(mesh):
    return jax.shard_map(
        body,
        mesh=mesh,
        in_specs=(P("ctx", "tp"), P(("ctx", "tp"), None), P(("ctx", "tp"), None), P("ctx", "tp"), P()),
        out_specs=(P("ctx", "tp"), P("ctx", "tp"), P(("ctx", "tp"), None), P(("ctx", "tp"), None)),
        check_vma=False,
    )
```

```python
import functools
import math

import jax
import jax.numpy as jnp
from jax import lax
from jax.experimental import pallas as pl
from jax.experimental.pallas import tpu as pltpu
from jax.sharding import PartitionSpec as P

D = 128
T = 256
W = 8
H = 8
NX = 4
ND = 8
ROWS = T // ND
SCALE = 1.0 / math.sqrt(D)
C2 = SCALE * math.log2(math.e)
BIG = 1e30
NT = (((1,), (1,)), ((), ()))
f32 = jnp.float32
bf16 = jnp.bfloat16
MESH = pl.DeviceIdType.MESH


KEYS = slice(0, T)
VALUES = slice(T, 2 * T)


def doc_rows(lens_ref):
    n = lens_ref.shape[1]
    sub = lax.broadcasted_iota(jnp.int32, (128, n), 0)
    lane = lax.broadcasted_iota(jnp.int32, (128, n), 1)
    lens = jnp.broadcast_to(lens_ref[...].astype(f32), (128, n))
    st = jnp.sum(jnp.where(lane < sub, lens, 0.0), axis=1, keepdims=True)
    en = jnp.sum(jnp.where(lane <= sub, lens, 0.0), axis=1, keepdims=True)
    st = jnp.transpose(jnp.broadcast_to(st, (128, 128)))
    en = jnp.transpose(jnp.broadcast_to(en, (128, 128)))
    last = lax.broadcasted_iota(jnp.int32, (128, 128), 1) == 127
    st = jnp.where(last, -1e9, st)
    en = jnp.where(last, 0.0, en)
    return st[0:1], en[0:1]


def kernel(
    nctx, lens_hbm, q_hbm, g_hbm, k_hbm, v_hbm, o_ref, dq_ref, dk_ref, dv_ref,
    lens_ref, q_ref, g_ref, kv, gb, pst, xst, zst, own, fin, kg, vg,
    qa, kb, three, qall, g2all, dall, kT, vT, m_ref, s_ref, p_ref, ds_ref,
    lsem, asend, arecv, zsend, zrecv, xsend, xrecv, psend, precv,
):
    i = lax.axis_index("ctx")
    me = lax.axis_index("tp")
    core = lax.rem(i, 2)
    x = lax.rem(lax.div(i, 2), NX)
    row = i - lax.rem(i, 2 * NX)
    base = lax.rem(i, 2 * NX)
    partner = i + 1 - 2 * core
    up = lax.rem(i + 2 * NX, nctx)
    down = lax.rem(i + nctx - 2 * NX, nctx)
    z = lax.div(i, 2 * NX)
    not_first = z > 0
    not_last = z < nctx // (2 * NX) - 1

    def chip(j):
        return row + lax.rem(base + 2 * j, 2 * NX)

    def peer(d):
        return lax.rem(me + d, ND)

    def remote(src, dst, send, recv, who):
        return pltpu.make_async_remote_copy(
            src_ref=src, dst_ref=dst, send_sem=send, recv_sem=recv, device_id=who, device_id_type=MESH
        )

    own_col = pl.ds(pl.multiple_of(me * D, D), D)
    own_row = [pl.ds(pl.multiple_of(half * T + me * ROWS, ROWS), ROWS) for half in (0, 1)]
    source = (k_hbm, v_hbm)
    loads = [pltpu.make_async_copy(q_hbm, q_ref, lsem.at[0]), pltpu.make_async_copy(g_hbm, g_ref, lsem.at[1])]
    for half in (0, 1):
        loads.append(
            pltpu.make_async_copy(source[half].at[:, own_col], kv.at[0, own_row[half]], lsem.at[2 + half])
        )
    loads.append(pltpu.make_async_copy(lens_hbm, lens_ref, lsem.at[4]))
    for copy in loads:
        copy.start()

    barrier = pltpu.get_barrier_semaphore()
    greeted = [(i, peer(d)) for d in range(1, ND)]
    greeted += [(c, me) for c in (partner, chip(1), chip(2), chip(3))]
    for who in greeted:
        pl.semaphore_signal(barrier, inc=1, device_id=who, device_id_type=MESH)
    pl.when(not_first)(
        lambda: pl.semaphore_signal(barrier, inc=1, device_id=(down, me), device_id_type=MESH)
    )
    pl.semaphore_wait(barrier, len(greeted) + jnp.where(not_last, 1, 0))

    spread = [[], []]
    for half in (0, 1):
        for d in range(1, ND):
            col = pl.ds(pl.multiple_of(peer(d) * D, D), D)
            copy = remote(
                source[half].at[:, col], kv.at[0, own_row[half]], asend.at[half, d], arecv.at[half, d], (i, peer(d))
            )
            copy.start()
            spread[half].append(copy)

    @pl.when(jnp.logical_not(not_first))
    def _():
        kv[8] = jnp.zeros((2 * T, D), bf16)

    @pl.when(jnp.logical_not(not_last))
    def _():
        zst[...] = jnp.zeros(zst.shape, bf16)

    loads[4].wait()
    lo, hi = doc_rows(lens_ref)
    pos0 = (i * T).astype(f32)
    sub = lax.broadcasted_iota(jnp.int32, (T, D), 0).astype(f32)
    lane = lax.broadcasted_iota(jnp.int32, (T, D), 1)
    qpos = pos0 + sub
    qa[...] = jnp.where((qpos >= lo) & (qpos < hi), 0.0, -BIG).astype(bf16)
    three[...] = jnp.where(lane < 3, 1.0, 0.0).astype(bf16)
    for j in range(W):
        kpos = qpos - j * T
        kb[j * T : (j + 1) * T] = jnp.where((kpos >= lo) & (kpos < hi), 1.0, 0.0).astype(bf16)
    vT[D:] = jnp.ones((16, W * T), bf16)
    m_ref[...] = jnp.full(m_ref.shape, -3e38, f32)
    loads[0].wait()
    loads[1].wait()
    for h in range(H):
        qall[h * T : (h + 1) * T] = q_ref[:, h * D : (h + 1) * D]

    half_of = (KEYS, VALUES)

    def zcopy(half):
        part = half_of[half]
        return remote(kv.at[0, part], kv.at[8, part], zsend.at[half], zrecv.at[half], (up, me))

    def xcopy(j, half):
        part = half_of[half]
        src = jnp.where(x + j < NX, 0, 8)
        return remote(kv.at[src, part], kv.at[2 * j, part], xsend.at[half, j], xrecv.at[half, j], (chip(j), me))

    def share(m, half):
        part = half_of[half]
        return remote(
            kv.at[2 * (m + core), part], kv.at[2 * m + 1, part], psend.at[half, m], precv.at[half, m], (partner, me)
        )

    for half in (0, 1):
        loads[2 + half].wait()
        for copy in spread[half]:
            copy.wait()
        pl.when(not_last)(zcopy(half).start)
        for j in (1, 3, 2):
            pl.when(x + j < NX)(xcopy(j, half).start)
        pl.when(core == 0)(lambda half=half: share(0, half).start())

    def scores(j):
        rows = slice(j * T, (j + 1) * T)
        keys = kv[j, KEYS]
        kT[:, rows] = jnp.transpose(keys)
        left = jnp.concatenate([keys, kb[rows]], axis=1)
        for h in range(H):
            cols = slice(h * T, (h + 1) * T)
            right = jnp.concatenate([qall[cols], qa[...]], axis=1)
            s = lax.dot_general(left, right, NT, preferred_element_type=f32)
            if j == 0:
                r = lax.broadcasted_iota(jnp.int32, (T, T), 0)
                c = lax.broadcasted_iota(jnp.int32, (T, T), 1)
                s = jnp.where(r <= c, s, -BIG)
            s_ref[rows, cols] = s
            m_ref[:, cols] = jnp.maximum(m_ref[:, cols], jnp.max(s.reshape(T // 8, 8, T), axis=0))

    scores(0)
    for half in (0, 1):
        pl.when(not_first)(zcopy(half).wait_recv)
        for j in (1, 3, 2):
            pl.when(x + j >= NX)(xcopy(j, half).start)
        pl.when(core == 1)(lambda half=half: share(3, half).start())
    for j in (1, 3, 2):
        xcopy(j, 0).wait_recv()
        share(j - core, 0).start()
        scores(2 * j)
    for j in (1, 3, 2):
        xcopy(j, 1).wait_recv()
        share(j - core, 1).start()
    for m in range(4):
        share(m, 0).wait()
        scores(2 * m + 1)
    for m in range(4):
        share(m, 1).wait()
    for half in (0, 1):
        pl.when(not_last)(zcopy(half).wait_send)
        for j in (1, 3, 2):
            xcopy(j, half).wait_send()
    for j in range(W):
        vT[:D, j * T : (j + 1) * T] = jnp.transpose(kv[j, VALUES])

    def weigh(h):
        cols = slice(h * T, (h + 1) * T)
        top = jnp.max(m_ref[:, cols], axis=0, keepdims=True)
        for j in range(W):
            rows = slice(j * T, (j + 1) * T)
            p_ref[rows, cols] = jnp.exp2((s_ref[rows, cols] - top) * C2).astype(bf16)

    def attend(h):
        cols = slice(h * T, (h + 1) * T)
        col = slice(h * D, (h + 1) * D)
        ot = jnp.dot(vT[...], p_ref[:, cols], preferred_element_type=f32)
        o = jnp.transpose(ot[:D])
        inv = jnp.transpose(1.0 / ot[D : D + 8])[:, 0:1]
        ob = (o * inv).astype(bf16)
        o_ref[:, col] = ob
        gf = g_ref[:, col].astype(f32)
        delta = jnp.sum(ob.astype(f32) * gf, axis=1, keepdims=True)
        rs = inv * SCALE
        g2all[cols] = (gf * rs).astype(bf16)
        dl = -delta * rs
        d1 = dl.astype(bf16).astype(f32)
        r1 = dl - d1
        d2 = r1.astype(bf16).astype(f32)
        d3 = r1 - d2
        dall[cols] = jnp.where(lane == 0, d1, jnp.where(lane == 1, d2, jnp.where(lane == 2, d3, 0.0))).astype(bf16)

    for stage in range(0, H + 2, 2):

        @pl.when(i >= 0)
        def _(stage=stage):
            for h in (stage, stage + 1):
                if h < H:
                    weigh(h)
                if h >= 2:
                    attend(h - 2)

    def value_gradient(j):
        rows = slice(j * T, (j + 1) * T)
        return jnp.dot(p_ref[rows], g2all[...], preferred_element_type=f32) * (1.0 / SCALE)

    def key_gradient(j):
        rows = slice(j * T, (j + 1) * T)
        left = jnp.concatenate([kv[j, VALUES], three[...]], axis=1)
        dk = None
        for part in range(2):
            for h in range(part * H // 2, (part + 1) * H // 2):
                cols = slice(h * T, (h + 1) * T)
                right = jnp.concatenate([g2all[cols], dall[cols]], axis=1)
                dp = lax.dot_general(left, right, NT, preferred_element_type=f32)
                ds_ref[rows, cols] = (p_ref[rows, cols].astype(f32) * dp).astype(bf16)
            cols = slice(part * H // 2 * T, (part + 1) * H // 2 * T)
            piece = jnp.dot(ds_ref[rows, cols], qall[cols], preferred_element_type=f32)
            dk = piece if dk is None else dk + piece
        return dk

    gradient = (key_gradient, value_gradient)

    def query_gradient(h):
        cols = slice(h * T, (h + 1) * T)
        dqt = jnp.dot(kT[...], ds_ref[:, cols], preferred_element_type=f32)
        dq_ref[:, h * D : (h + 1) * D] = jnp.transpose(dqt).astype(bf16)

    def give(m, half):
        part = half_of[half]
        return remote(
            gb.at[2 * m + 1, part], pst.at[m, part], psend.at[2 + half, m], precv.at[2 + half, m], (partner, me)
        )

    quarter_of = [slice(e * T // 2, (e + 1) * T // 2) for e in range(4)]

    def xback(j, e):
        part = quarter_of[e]
        return remote(
            gb.at[2 * j, part], xst.at[j, part], xsend.at[2 + e, j], xrecv.at[2 + e, j], (chip(NX - j), me)
        )

    def zback(e):
        part = quarter_of[e]
        return remote(gb.at[8, part], zst.at[part], zsend.at[2 + e], zrecv.at[2 + e], (down, me))

    def odd(j, half):
        gb[j, half_of[half]] = gradient[half](j).astype(bf16)
        give(j // 2, half).start()

    def even(j, half):
        part = half_of[half]
        grad = gradient[half](j)
        for m in {6: (3, 2), 4: (1,), 2: (0,)}[j]:
            give(m, half).wait()
        gb[j, part] = (grad + pst[j // 2 - core, part].astype(f32)).astype(bf16)
        for e in (2 * half, 2 * half + 1):
            xback(j // 2, e).start()

    first_part = jnp.where(core == 0, 1.0, 0.0)
    last_part = jnp.where(core == 1, 1.0, 0.0)

    def fold(e):
        part = quarter_of[e]
        total = own[part] + pst[0, part].astype(f32) * first_part
        prev = pst[3, part].astype(f32) * last_part
        for j in (3, 2, 1):
            xback(j, e).wait()
            mine = jnp.where(x + j < NX, 1.0, 0.0)
            got = xst[j, part].astype(f32)
            total += got * mine
            prev += got * (1.0 - mine)
        gb[8, part] = prev.astype(bf16)
        pl.when(not_first)(zback(e).start)
        own[part] = total

    out = (kg, vg)

    def deliver(half, d):
        rows = pl.ds(pl.multiple_of(half * T + peer(d) * ROWS, ROWS), ROWS)
        return remote(
            fin.at[rows], out[half].at[:, own_col], asend.at[2 + half, d], arecv.at[2 + half, d], (i, peer(d))
        )

    def finish(e):
        part = quarter_of[e]
        half = e // 2
        pl.when(not_last)(zback(e).wait_recv)
        fin[part] = (own[part] + zst[part].astype(f32)).astype(bf16)
        for d in range(1, ND):
            here = lax.div(peer(d), ND // 2) == e % 2
            pl.when(here)(deliver(half, d).start)

    for j in (7, 5, 3, 1):
        odd(j, 1)
    for j in (6, 4, 2):
        even(j, 1)
    own[VALUES] = value_gradient(0)
    for j in (7, 5, 3, 1):
        odd(j, 0)
    even(6, 0)
    fold(2)
    fold(3)
    for j in (4, 2):
        even(j, 0)
    own[KEYS] = key_gradient(0)
    for h in range(4):
        query_gradient(h)
    finish(2)
    finish(3)
    for h in range(4, 6):
        query_gradient(h)
    fold(0)
    fold(1)
    for h in range(6, 8):
        query_gradient(h)
    finish(0)
    finish(1)
    kg[:, own_col] = fin[own_row[0]]
    vg[:, own_col] = fin[own_row[1]]
    for e in range(4):
        pl.when(not_first)(zback(e).wait_send)
    for half in (1, 0):
        for d in range(1, ND):
            deliver(half, d).wait()
    dk_ref[...] = kg[...]
    dv_ref[...] = vg[...]


def write_kernel(o_in, dq_in, dk_in, dv_in, o_out, dq_out, dk_out, dv_out, sem):
    pairs = ((o_in, o_out), (dq_in, dq_out), (dk_in, dk_out), (dv_in, dv_out))
    copies = [pltpu.make_async_copy(a, b, sem.at[n]) for n, (a, b) in enumerate(pairs)]
    for copy in copies:
        copy.start()
    for copy in copies:
        copy.wait()


def body(queries, key_vectors, value_vectors, output_gradient, doc_lengths):
    vm = pl.BlockSpec(memory_space=pltpu.VMEM)
    free = pl.BlockSpec(memory_space=pl.ANY)
    dma = pltpu.SemaphoreType.DMA
    vmem = pltpu.VMEM
    big = jax.ShapeDtypeStruct((T, H * D), bf16)
    small = jax.ShapeDtypeStruct((ROWS, ND * D), bf16)
    arrays = [
        pltpu.with_memory_space_constraint(a, pltpu.HBM)
        for a in (doc_lengths.reshape(1, -1), queries, output_gradient, key_vectors, value_vectors)
    ]
    parts = pl.pallas_call(
        functools.partial(kernel, lax.axis_size("ctx")),
        out_shape=(big, big, small, small),
        in_specs=[free] * 5,
        out_specs=(vm,) * 4,
        scratch_shapes=[
            vmem((1, doc_lengths.shape[0]), jnp.int32),
            vmem((T, H * D), bf16),
            vmem((T, H * D), bf16),
            vmem((9, 2 * T, D), bf16),
            vmem((9, 2 * T, D), bf16),
            vmem((4, 2 * T, D), bf16),
            vmem((4, 2 * T, D), bf16),
            vmem((2 * T, D), bf16),
            vmem((2 * T, D), f32),
            vmem((2 * T, D), bf16),
            vmem((ROWS, ND * D), bf16),
            vmem((ROWS, ND * D), bf16),
            vmem((T, D), bf16),
            vmem((W * T, D), bf16),
            vmem((T, D), bf16),
            vmem((H * T, D), bf16),
            vmem((H * T, D), bf16),
            vmem((H * T, D), bf16),
            vmem((D, W * T), bf16),
            vmem((D + 16, W * T), bf16),
            vmem((8, H * T), f32),
            vmem((W * T, H * T), f32),
            vmem((W * T, H * T), bf16),
            vmem((W * T, H * T), bf16),
            dma((5,)),
            dma((4, ND)),
            dma((4, ND)),
            dma((6,)),
            dma((6,)),
            dma((6, NX)),
            dma((6, NX)),
            dma((4, 4)),
            dma((4, 4)),
        ],
        compiler_params=pltpu.CompilerParams(
            collective_id=0, has_side_effects=True, vmem_limit_bytes=52 << 20
        ),
        name="attention",
    )(*arrays)
    return pl.pallas_call(
        write_kernel,
        out_shape=(big, big, small, small),
        in_specs=[free] * 4,
        out_specs=(free,) * 4,
        scratch_shapes=[dma((4,))],
        compiler_params=pltpu.CompilerParams(vmem_limit_bytes=2 << 20),
        name="write",
    )(*parts)


def solution(mesh):
    return jax.shard_map(
        body,
        mesh=mesh,
        in_specs=(P("ctx", "tp"), P(("ctx", "tp"), None), P(("ctx", "tp"), None), P("ctx", "tp"), P()),
        out_specs=(P("ctx", "tp"), P("ctx", "tp"), P(("ctx", "tp"), None), P(("ctx", "tp"), None)),
        check_vma=False,
    )
```

```python
import functools
import math

import jax
import jax.numpy as jnp
from jax import lax
from jax.experimental import pallas as pl
from jax.experimental.pallas import tpu as pltpu
from jax.sharding import PartitionSpec as P

D = 128
T = 256
W = 8
H = 8
NX = 4
ND = 8
ROWS = T // ND
SCALE = 1.0 / math.sqrt(D)
C2 = SCALE * math.log2(math.e)
BIG = 1e30
NT = (((1,), (1,)), ((), ()))
f32 = jnp.float32
bf16 = jnp.bfloat16
MESH = pl.DeviceIdType.MESH


KEYS = slice(0, T)
VALUES = slice(T, 2 * T)


def doc_rows(lens_ref):
    n = lens_ref.shape[1]
    sub = lax.broadcasted_iota(jnp.int32, (128, n), 0)
    lane = lax.broadcasted_iota(jnp.int32, (128, n), 1)
    lens = jnp.broadcast_to(lens_ref[...].astype(f32), (128, n))
    st = jnp.sum(jnp.where(lane < sub, lens, 0.0), axis=1, keepdims=True)
    en = jnp.sum(jnp.where(lane <= sub, lens, 0.0), axis=1, keepdims=True)
    st = jnp.transpose(jnp.broadcast_to(st, (128, 128)))
    en = jnp.transpose(jnp.broadcast_to(en, (128, 128)))
    last = lax.broadcasted_iota(jnp.int32, (128, 128), 1) == 127
    st = jnp.where(last, -1e9, st)
    en = jnp.where(last, 0.0, en)
    return st[0:1], en[0:1]


def kernel(
    nctx, lens_hbm, q_hbm, g_hbm, k_hbm, v_hbm, o_ref, dq_ref, dk_ref, dv_ref,
    lens_ref, q_ref, g_ref, kv, gb, pst, xst, zst, own, fin, kg, vg,
    qa, kb, three, qall, g2all, dall, kT, vT, m_ref, s_ref, p_ref, ds_ref,
    lsem, asend, arecv, zsend, zrecv, xsend, xrecv, psend, precv,
):
    i = lax.axis_index("ctx")
    me = lax.axis_index("tp")
    core = lax.rem(i, 2)
    x = lax.rem(lax.div(i, 2), NX)
    row = i - lax.rem(i, 2 * NX)
    base = lax.rem(i, 2 * NX)
    partner = i + 1 - 2 * core
    up = lax.rem(i + 2 * NX, nctx)
    down = lax.rem(i + nctx - 2 * NX, nctx)
    z = lax.div(i, 2 * NX)
    not_first = z > 0
    not_last = z < nctx // (2 * NX) - 1

    def chip(j):
        return row + lax.rem(base + 2 * j, 2 * NX)

    def peer(d):
        return lax.rem(me + d, ND)

    def remote(src, dst, send, recv, who):
        return pltpu.make_async_remote_copy(
            src_ref=src, dst_ref=dst, send_sem=send, recv_sem=recv, device_id=who, device_id_type=MESH
        )

    own_col = pl.ds(pl.multiple_of(me * D, D), D)
    own_row = [pl.ds(pl.multiple_of(half * T + me * ROWS, ROWS), ROWS) for half in (0, 1)]
    source = (k_hbm, v_hbm)
    loads = [pltpu.make_async_copy(q_hbm, q_ref, lsem.at[0]), pltpu.make_async_copy(g_hbm, g_ref, lsem.at[1])]
    for half in (0, 1):
        loads.append(
            pltpu.make_async_copy(source[half].at[:, own_col], kv.at[0, own_row[half]], lsem.at[2 + half])
        )
    loads.append(pltpu.make_async_copy(lens_hbm, lens_ref, lsem.at[4]))
    for copy in loads:
        copy.start()

    barrier = pltpu.get_barrier_semaphore()
    greeted = [(i, peer(d)) for d in range(1, ND)]
    greeted += [(c, me) for c in (partner, chip(1), chip(2), chip(3))]
    for who in greeted:
        pl.semaphore_signal(barrier, inc=1, device_id=who, device_id_type=MESH)
    pl.when(not_first)(
        lambda: pl.semaphore_signal(barrier, inc=1, device_id=(down, me), device_id_type=MESH)
    )
    pl.semaphore_wait(barrier, len(greeted) + jnp.where(not_last, 1, 0))

    spread = [[], []]
    for half in (0, 1):
        for d in range(1, ND):
            col = pl.ds(pl.multiple_of(peer(d) * D, D), D)
            copy = remote(
                source[half].at[:, col], kv.at[0, own_row[half]], asend.at[half, d], arecv.at[half, d], (i, peer(d))
            )
            copy.start()
            spread[half].append(copy)

    @pl.when(jnp.logical_not(not_first))
    def _():
        kv[8] = jnp.zeros((2 * T, D), bf16)

    @pl.when(jnp.logical_not(not_last))
    def _():
        zst[...] = jnp.zeros(zst.shape, bf16)

    loads[4].wait()
    lo, hi = doc_rows(lens_ref)
    pos0 = (i * T).astype(f32)
    sub = lax.broadcasted_iota(jnp.int32, (T, D), 0).astype(f32)
    lane = lax.broadcasted_iota(jnp.int32, (T, D), 1)
    qpos = pos0 + sub
    qa[...] = jnp.where((qpos >= lo) & (qpos < hi), 0.0, -BIG).astype(bf16)
    three[...] = jnp.where(lane < 3, 1.0, 0.0).astype(bf16)
    for j in range(W):
        kpos = qpos - j * T
        kb[j * T : (j + 1) * T] = jnp.where((kpos >= lo) & (kpos < hi), 1.0, 0.0).astype(bf16)
    vT[D:] = jnp.ones((16, W * T), bf16)
    m_ref[...] = jnp.full(m_ref.shape, -3e38, f32)
    loads[0].wait()
    loads[1].wait()
    for h in range(H):
        qall[h * T : (h + 1) * T] = q_ref[:, h * D : (h + 1) * D]

    half_of = (KEYS, VALUES)

    def zcopy(half):
        part = half_of[half]
        return remote(kv.at[0, part], kv.at[8, part], zsend.at[half], zrecv.at[half], (up, me))

    def xcopy(j, half):
        part = half_of[half]
        src = jnp.where(x + j < NX, 0, 8)
        return remote(kv.at[src, part], kv.at[2 * j, part], xsend.at[half, j], xrecv.at[half, j], (chip(j), me))

    def share(m, half):
        part = half_of[half]
        return remote(
            kv.at[2 * (m + core), part], kv.at[2 * m + 1, part], psend.at[half, m], precv.at[half, m], (partner, me)
        )

    for half in (0, 1):
        loads[2 + half].wait()
        for copy in spread[half]:
            copy.wait()
        pl.when(not_last)(zcopy(half).start)
        for j in (1, 3, 2):
            pl.when(x + j < NX)(xcopy(j, half).start)
        pl.when(core == 0)(lambda half=half: share(0, half).start())

    def scores(j):
        rows = slice(j * T, (j + 1) * T)
        keys = kv[j, KEYS]
        kT[:, rows] = jnp.transpose(keys)
        left = jnp.concatenate([keys, kb[rows]], axis=1)
        for h in range(H):
            cols = slice(h * T, (h + 1) * T)
            right = jnp.concatenate([qall[cols], qa[...]], axis=1)
            s = lax.dot_general(left, right, NT, preferred_element_type=f32)
            if j == 0:
                r = lax.broadcasted_iota(jnp.int32, (T, T), 0)
                c = lax.broadcasted_iota(jnp.int32, (T, T), 1)
                s = jnp.where(r <= c, s, -BIG)
            s_ref[rows, cols] = s
            m_ref[:, cols] = jnp.maximum(m_ref[:, cols], jnp.max(s.reshape(T // 8, 8, T), axis=0))

    scores(0)
    for half in (0, 1):
        pl.when(not_first)(zcopy(half).wait_recv)
        for j in (1, 3, 2):
            pl.when(x + j >= NX)(xcopy(j, half).start)
        pl.when(core == 1)(lambda half=half: share(3, half).start())
    for j in (1, 3, 2):
        xcopy(j, 0).wait_recv()
        share(j - core, 0).start()
        scores(2 * j)
    for m in (0, 1):
        share(m, 0).wait()
        scores(2 * m + 1)
    for j in (1, 3, 2):
        xcopy(j, 1).wait_recv()
        share(j - core, 1).start()
    for m in (2, 3):
        share(m, 0).wait()
        scores(2 * m + 1)

    def weigh(h):
        cols = slice(h * T, (h + 1) * T)
        top = jnp.max(m_ref[:, cols], axis=0, keepdims=True)
        for j in range(W):
            rows = slice(j * T, (j + 1) * T)
            p_ref[rows, cols] = jnp.exp2((s_ref[rows, cols] - top) * C2).astype(bf16)

    def attend(h):
        cols = slice(h * T, (h + 1) * T)
        col = slice(h * D, (h + 1) * D)
        ot = jnp.dot(vT[...], p_ref[:, cols], preferred_element_type=f32)
        o = jnp.transpose(ot[:D])
        inv = jnp.transpose(1.0 / ot[D : D + 8])[:, 0:1]
        ob = (o * inv).astype(bf16)
        o_ref[:, col] = ob
        gf = g_ref[:, col].astype(f32)
        delta = jnp.sum(ob.astype(f32) * gf, axis=1, keepdims=True)
        rs = inv * SCALE
        g2all[cols] = (gf * rs).astype(bf16)
        dl = -delta * rs
        d1 = dl.astype(bf16).astype(f32)
        r1 = dl - d1
        d2 = r1.astype(bf16).astype(f32)
        d3 = r1 - d2
        dall[cols] = jnp.where(lane == 0, d1, jnp.where(lane == 1, d2, jnp.where(lane == 2, d3, 0.0))).astype(bf16)

    for stage in range(0, H + 2, 2):
        if stage == 2:
            for m in range(4):
                share(m, 1).wait()
            for j in range(W):
                vT[:D, j * T : (j + 1) * T] = jnp.transpose(kv[j, VALUES])

        @pl.when(i >= 0)
        def _(stage=stage):
            for h in (stage, stage + 1):
                if h < H:
                    weigh(h)
                if h >= 2:
                    attend(h - 2)

    def value_gradient(j):
        rows = slice(j * T, (j + 1) * T)
        return jnp.dot(p_ref[rows], g2all[...], preferred_element_type=f32) * (1.0 / SCALE)

    def key_gradient(j):
        rows = slice(j * T, (j + 1) * T)
        left = jnp.concatenate([kv[j, VALUES], three[...]], axis=1)
        dk = None
        for part in range(2):
            for h in range(part * H // 2, (part + 1) * H // 2):
                cols = slice(h * T, (h + 1) * T)
                right = jnp.concatenate([g2all[cols], dall[cols]], axis=1)
                dp = lax.dot_general(left, right, NT, preferred_element_type=f32)
                ds_ref[rows, cols] = (p_ref[rows, cols].astype(f32) * dp).astype(bf16)
            cols = slice(part * H // 2 * T, (part + 1) * H // 2 * T)
            piece = jnp.dot(ds_ref[rows, cols], qall[cols], preferred_element_type=f32)
            dk = piece if dk is None else dk + piece
        return dk

    gradient = (key_gradient, value_gradient)

    def query_gradient(h):
        cols = slice(h * T, (h + 1) * T)
        dqt = jnp.dot(kT[...], ds_ref[:, cols], preferred_element_type=f32)
        dq_ref[:, h * D : (h + 1) * D] = jnp.transpose(dqt).astype(bf16)

    def give(m, half):
        part = half_of[half]
        return remote(
            gb.at[2 * m + 1, part], pst.at[m, part], psend.at[2 + half, m], precv.at[2 + half, m], (partner, me)
        )

    quarter_of = [slice(e * T // 2, (e + 1) * T // 2) for e in range(4)]

    def xback(j, e):
        part = quarter_of[e]
        return remote(
            gb.at[2 * j, part], xst.at[j, part], xsend.at[2 + e, j], xrecv.at[2 + e, j], (chip(NX - j), me)
        )

    def zback(e):
        part = quarter_of[e]
        return remote(gb.at[8, part], zst.at[part], zsend.at[2 + e], zrecv.at[2 + e], (down, me))

    def odd(j, half):
        gb[j, half_of[half]] = gradient[half](j).astype(bf16)
        give(j // 2, half).start()

    def even(j, half):
        part = half_of[half]
        grad = gradient[half](j)
        for m in {4: (2, 1), 6: (3,), 2: (0,)}[j]:
            give(m, half).wait()
        gb[j, part] = (grad + pst[j // 2 - core, part].astype(f32)).astype(bf16)
        for e in (2 * half, 2 * half + 1):
            xback(j // 2, e).start()

    first_part = jnp.where(core == 0, 1.0, 0.0)
    last_part = jnp.where(core == 1, 1.0, 0.0)

    def fold(e):
        part = quarter_of[e]
        total = own[part] + pst[0, part].astype(f32) * first_part
        prev = pst[3, part].astype(f32) * last_part
        for j in (2, 3, 1):
            xback(j, e).wait()
            mine = jnp.where(x + j < NX, 1.0, 0.0)
            got = xst[j, part].astype(f32)
            total += got * mine
            prev += got * (1.0 - mine)
        gb[8, part] = prev.astype(bf16)
        pl.when(not_first)(zback(e).start)
        own[part] = total

    out = (kg, vg)

    def deliver(half, d):
        rows = pl.ds(pl.multiple_of(half * T + peer(d) * ROWS, ROWS), ROWS)
        return remote(
            fin.at[rows], out[half].at[:, own_col], asend.at[2 + half, d], arecv.at[2 + half, d], (i, peer(d))
        )

    def finish(e):
        part = quarter_of[e]
        half = e // 2
        pl.when(not_last)(zback(e).wait_recv)
        fin[part] = (own[part] + zst[part].astype(f32)).astype(bf16)
        for d in range(1, ND):
            here = lax.div(peer(d), ND // 2) == e % 2
            pl.when(here)(deliver(half, d).start)

    for j in (5, 3, 7, 1):
        odd(j, 1)
    for j in (4, 6, 2):
        even(j, 1)
    own[VALUES] = value_gradient(0)
    odd(5, 0)
    odd(3, 0)
    odd(7, 0)
    even(4, 0)
    odd(1, 0)
    even(6, 0)
    fold(2)
    fold(3)
    even(2, 0)
    own[KEYS] = key_gradient(0)
    for h in range(4):
        query_gradient(h)
    fold(0)
    fold(1)
    finish(2)
    finish(3)
    for h in range(4, 8):
        query_gradient(h)
    finish(0)
    finish(1)
    kg[:, own_col] = fin[own_row[0]]
    vg[:, own_col] = fin[own_row[1]]
    for e in range(4):
        pl.when(not_first)(zback(e).wait_send)
    for half in (0, 1):
        pl.when(not_last)(zcopy(half).wait_send)
        for j in (1, 3, 2):
            xcopy(j, half).wait_send()
    for half in (1, 0):
        for d in range(1, ND):
            deliver(half, d).wait()
    dk_ref[...] = kg[...]
    dv_ref[...] = vg[...]


def write_kernel(o_in, dq_in, dk_in, dv_in, o_out, dq_out, dk_out, dv_out, sem):
    pairs = ((o_in, o_out), (dq_in, dq_out), (dk_in, dk_out), (dv_in, dv_out))
    copies = [pltpu.make_async_copy(a, b, sem.at[n]) for n, (a, b) in enumerate(pairs)]
    for copy in copies:
        copy.start()
    for copy in copies:
        copy.wait()


def body(queries, key_vectors, value_vectors, output_gradient, doc_lengths):
    vm = pl.BlockSpec(memory_space=pltpu.VMEM)
    free = pl.BlockSpec(memory_space=pl.ANY)
    dma = pltpu.SemaphoreType.DMA
    vmem = pltpu.VMEM
    big = jax.ShapeDtypeStruct((T, H * D), bf16)
    small = jax.ShapeDtypeStruct((ROWS, ND * D), bf16)
    arrays = [
        pltpu.with_memory_space_constraint(a, pltpu.HBM)
        for a in (doc_lengths.reshape(1, -1), queries, output_gradient, key_vectors, value_vectors)
    ]
    parts = pl.pallas_call(
        functools.partial(kernel, lax.axis_size("ctx")),
        out_shape=(big, big, small, small),
        in_specs=[free] * 5,
        out_specs=(vm,) * 4,
        scratch_shapes=[
            vmem((1, doc_lengths.shape[0]), jnp.int32),
            vmem((T, H * D), bf16),
            vmem((T, H * D), bf16),
            vmem((9, 2 * T, D), bf16),
            vmem((9, 2 * T, D), bf16),
            vmem((4, 2 * T, D), bf16),
            vmem((4, 2 * T, D), bf16),
            vmem((2 * T, D), bf16),
            vmem((2 * T, D), f32),
            vmem((2 * T, D), bf16),
            vmem((ROWS, ND * D), bf16),
            vmem((ROWS, ND * D), bf16),
            vmem((T, D), bf16),
            vmem((W * T, D), bf16),
            vmem((T, D), bf16),
            vmem((H * T, D), bf16),
            vmem((H * T, D), bf16),
            vmem((H * T, D), bf16),
            vmem((D, W * T), bf16),
            vmem((D + 16, W * T), bf16),
            vmem((8, H * T), f32),
            vmem((W * T, H * T), f32),
            vmem((W * T, H * T), bf16),
            vmem((W * T, H * T), bf16),
            dma((5,)),
            dma((4, ND)),
            dma((4, ND)),
            dma((6,)),
            dma((6,)),
            dma((6, NX)),
            dma((6, NX)),
            dma((4, 4)),
            dma((4, 4)),
        ],
        compiler_params=pltpu.CompilerParams(
            collective_id=0, has_side_effects=True, vmem_limit_bytes=52 << 20
        ),
        name="attention",
    )(*arrays)
    return pl.pallas_call(
        write_kernel,
        out_shape=(big, big, small, small),
        in_specs=[free] * 4,
        out_specs=(free,) * 4,
        scratch_shapes=[dma((4,))],
        compiler_params=pltpu.CompilerParams(vmem_limit_bytes=2 << 20),
        name="write",
    )(*parts)


def solution(mesh):
    return jax.shard_map(
        body,
        mesh=mesh,
        in_specs=(P("ctx", "tp"), P(("ctx", "tp"), None), P(("ctx", "tp"), None), P("ctx", "tp"), P()),
        out_specs=(P("ctx", "tp"), P("ctx", "tp"), P(("ctx", "tp"), None), P(("ctx", "tp"), None)),
        check_vma=False,
    )
```

```python
import functools
import math

import jax
import jax.numpy as jnp
from jax import lax
from jax.experimental import pallas as pl
from jax.experimental.pallas import tpu as pltpu
from jax.sharding import PartitionSpec as P

D = 128
T = 256
W = 8
H = 8
NX = 4
ND = 8
ROWS = T // ND
SCALE = 1.0 / math.sqrt(D)
C2 = SCALE * math.log2(math.e)
BIG = 1e30
NT = (((1,), (1,)), ((), ()))
f32 = jnp.float32
bf16 = jnp.bfloat16
MESH = pl.DeviceIdType.MESH


KEYS = slice(0, T)
VALUES = slice(T, 2 * T)


def doc_rows(lens_ref):
    n = lens_ref.shape[1]
    sub = lax.broadcasted_iota(jnp.int32, (128, n), 0)
    lane = lax.broadcasted_iota(jnp.int32, (128, n), 1)
    lens = jnp.broadcast_to(lens_ref[...].astype(f32), (128, n))
    st = jnp.sum(jnp.where(lane < sub, lens, 0.0), axis=1, keepdims=True)
    en = jnp.sum(jnp.where(lane <= sub, lens, 0.0), axis=1, keepdims=True)
    st = jnp.transpose(jnp.broadcast_to(st, (128, 128)))
    en = jnp.transpose(jnp.broadcast_to(en, (128, 128)))
    last = lax.broadcasted_iota(jnp.int32, (128, 128), 1) == 127
    st = jnp.where(last, -1e9, st)
    en = jnp.where(last, 0.0, en)
    return st[0:1], en[0:1]


def kernel(
    nctx, lens_hbm, q_hbm, g_hbm, k_hbm, v_hbm, o_ref, dq_ref, dk_ref, dv_ref,
    lens_ref, q_ref, g_ref, kv, gb, pst, xst, zst, own, fin, kg, vg,
    qa, kb, three, qall, g2all, dall, kT, vT, m_ref, s_ref, p_ref, ds_ref,
    lsem, asend, arecv, zsend, zrecv, xsend, xrecv, psend, precv,
):
    i = lax.axis_index("ctx")
    me = lax.axis_index("tp")
    core = lax.rem(i, 2)
    x = lax.rem(lax.div(i, 2), NX)
    row = i - lax.rem(i, 2 * NX)
    base = lax.rem(i, 2 * NX)
    partner = i + 1 - 2 * core
    up = lax.rem(i + 2 * NX, nctx)
    down = lax.rem(i + nctx - 2 * NX, nctx)
    z = lax.div(i, 2 * NX)
    not_first = z > 0
    not_last = z < nctx // (2 * NX) - 1

    def chip(j):
        return row + lax.rem(base + 2 * j, 2 * NX)

    def peer(d):
        return lax.rem(me + d, ND)

    def remote(src, dst, send, recv, who):
        return pltpu.make_async_remote_copy(
            src_ref=src, dst_ref=dst, send_sem=send, recv_sem=recv, device_id=who, device_id_type=MESH
        )

    own_col = pl.ds(pl.multiple_of(me * D, D), D)
    own_row = [pl.ds(pl.multiple_of(half * T + me * ROWS, ROWS), ROWS) for half in (0, 1)]
    source = (k_hbm, v_hbm)
    loads = [pltpu.make_async_copy(q_hbm, q_ref, lsem.at[0]), pltpu.make_async_copy(g_hbm, g_ref, lsem.at[1])]
    for half in (0, 1):
        loads.append(
            pltpu.make_async_copy(source[half].at[:, own_col], kv.at[0, own_row[half]], lsem.at[2 + half])
        )
    loads.append(pltpu.make_async_copy(lens_hbm, lens_ref, lsem.at[4]))
    for copy in loads:
        copy.start()

    barrier = pltpu.get_barrier_semaphore()
    greeted = [(i, peer(d)) for d in range(1, ND)]
    greeted += [(c, me) for c in (partner, chip(1), chip(2), chip(3))]
    for who in greeted:
        pl.semaphore_signal(barrier, inc=1, device_id=who, device_id_type=MESH)
    pl.when(not_first)(
        lambda: pl.semaphore_signal(barrier, inc=1, device_id=(down, me), device_id_type=MESH)
    )
    pl.semaphore_wait(barrier, len(greeted) + jnp.where(not_last, 1, 0))

    spread = [[], []]
    for half in (0, 1):
        for d in range(1, ND):
            col = pl.ds(pl.multiple_of(peer(d) * D, D), D)
            copy = remote(
                source[half].at[:, col], kv.at[0, own_row[half]], asend.at[half, d], arecv.at[half, d], (i, peer(d))
            )
            copy.start()
            spread[half].append(copy)

    @pl.when(jnp.logical_not(not_first))
    def _():
        kv[8] = jnp.zeros((2 * T, D), bf16)

    @pl.when(jnp.logical_not(not_last))
    def _():
        zst[...] = jnp.zeros(zst.shape, bf16)

    loads[4].wait()
    lo, hi = doc_rows(lens_ref)
    pos0 = (i * T).astype(f32)
    sub = lax.broadcasted_iota(jnp.int32, (T, D), 0).astype(f32)
    lane = lax.broadcasted_iota(jnp.int32, (T, D), 1)
    qpos = pos0 + sub
    qa[...] = jnp.where((qpos >= lo) & (qpos < hi), 0.0, -BIG).astype(bf16)
    three[...] = jnp.where(lane < 3, 1.0, 0.0).astype(bf16)
    for j in range(W):
        kpos = qpos - j * T
        kb[j * T : (j + 1) * T] = jnp.where((kpos >= lo) & (kpos < hi), 1.0, 0.0).astype(bf16)
    vT[D:] = jnp.ones((16, W * T), bf16)
    m_ref[...] = jnp.full(m_ref.shape, -3e38, f32)
    loads[0].wait()
    loads[1].wait()
    for h in range(H):
        qall[h * T : (h + 1) * T] = q_ref[:, h * D : (h + 1) * D]

    half_of = (KEYS, VALUES)

    def zcopy(half):
        part = half_of[half]
        return remote(kv.at[0, part], kv.at[8, part], zsend.at[half], zrecv.at[half], (up, me))

    def xcopy(j, half):
        part = half_of[half]
        src = jnp.where(x + j < NX, 0, 8)
        return remote(kv.at[src, part], kv.at[2 * j, part], xsend.at[half, j], xrecv.at[half, j], (chip(j), me))

    def share(m, half):
        part = half_of[half]
        return remote(
            kv.at[2 * (m + core), part], kv.at[2 * m + 1, part], psend.at[half, m], precv.at[half, m], (partner, me)
        )

    for half in (0, 1):
        loads[2 + half].wait()
        for copy in spread[half]:
            copy.wait()
        pl.when(not_last)(zcopy(half).start)
        for j in (1, 3, 2):
            pl.when(x + j < NX)(xcopy(j, half).start)
        pl.when(core == 0)(lambda half=half: share(0, half).start())

    def scores(j):
        rows = slice(j * T, (j + 1) * T)
        keys = kv[j, KEYS]
        kT[:, rows] = jnp.transpose(keys)
        left = jnp.concatenate([keys, kb[rows]], axis=1)
        for h in range(H):
            cols = slice(h * T, (h + 1) * T)
            right = jnp.concatenate([qall[cols], qa[...]], axis=1)
            s = lax.dot_general(left, right, NT, preferred_element_type=f32)
            if j == 0:
                r = lax.broadcasted_iota(jnp.int32, (T, T), 0)
                c = lax.broadcasted_iota(jnp.int32, (T, T), 1)
                s = jnp.where(r <= c, s, -BIG)
            s_ref[rows, cols] = s
            m_ref[:, cols] = jnp.maximum(m_ref[:, cols], jnp.max(s.reshape(T // 8, 8, T), axis=0))

    scores(0)
    for half in (0, 1):
        pl.when(not_first)(zcopy(half).wait_recv)
        for j in (1, 3, 2):
            pl.when(x + j >= NX)(xcopy(j, half).start)
        pl.when(core == 1)(lambda half=half: share(3, half).start())
    for j in (1, 3, 2):
        xcopy(j, 0).wait_recv()
        share(j - core, 0).start()
        scores(2 * j)
    for j in (1, 3, 2):
        xcopy(j, 1).wait_recv()
        share(j - core, 1).start()
    for m in range(4):
        share(m, 0).wait()
        scores(2 * m + 1)
    for m in range(4):
        share(m, 1).wait()
    for half in (0, 1):
        pl.when(not_last)(zcopy(half).wait_send)
        for j in (1, 3, 2):
            xcopy(j, half).wait_send()
    for j in range(W):
        vT[:D, j * T : (j + 1) * T] = jnp.transpose(kv[j, VALUES])

    def weigh(h):
        cols = slice(h * T, (h + 1) * T)
        top = jnp.max(m_ref[:, cols], axis=0, keepdims=True)
        for j in range(W):
            rows = slice(j * T, (j + 1) * T)
            p_ref[rows, cols] = jnp.exp2((s_ref[rows, cols] - top) * C2).astype(bf16)

    def attend(h):
        cols = slice(h * T, (h + 1) * T)
        col = slice(h * D, (h + 1) * D)
        ot = jnp.dot(vT[...], p_ref[:, cols], preferred_element_type=f32)
        o = jnp.transpose(ot[:D])
        inv = jnp.transpose(1.0 / ot[D : D + 8])[:, 0:1]
        ob = (o * inv).astype(bf16)
        o_ref[:, col] = ob
        gf = g_ref[:, col].astype(f32)
        delta = jnp.sum(ob.astype(f32) * gf, axis=1, keepdims=True)
        rs = inv * SCALE
        g2all[cols] = (gf * rs).astype(bf16)
        dl = -delta * rs
        d1 = dl.astype(bf16).astype(f32)
        r1 = dl - d1
        d2 = r1.astype(bf16).astype(f32)
        d3 = r1 - d2
        dall[cols] = jnp.where(lane == 0, d1, jnp.where(lane == 1, d2, jnp.where(lane == 2, d3, 0.0))).astype(bf16)

    for stage in range(0, H + 2, 2):

        @pl.when(i >= 0)
        def _(stage=stage):
            for h in (stage, stage + 1):
                if h < H:
                    weigh(h)
                if h >= 2:
                    attend(h - 2)

    def value_gradient(j):
        rows = slice(j * T, (j + 1) * T)
        return jnp.dot(p_ref[rows], g2all[...], preferred_element_type=f32) * (1.0 / SCALE)

    def key_gradient(j):
        rows = slice(j * T, (j + 1) * T)
        left = jnp.concatenate([kv[j, VALUES], three[...]], axis=1)
        dk = None
        for part in range(2):
            for h in range(part * H // 2, (part + 1) * H // 2):
                cols = slice(h * T, (h + 1) * T)
                right = jnp.concatenate([g2all[cols], dall[cols]], axis=1)
                dp = lax.dot_general(left, right, NT, preferred_element_type=f32)
                ds_ref[rows, cols] = (p_ref[rows, cols].astype(f32) * dp).astype(bf16)
            cols = slice(part * H // 2 * T, (part + 1) * H // 2 * T)
            piece = jnp.dot(ds_ref[rows, cols], qall[cols], preferred_element_type=f32)
            dk = piece if dk is None else dk + piece
        return dk

    gradient = (key_gradient, value_gradient)

    def query_gradient(h):
        cols = slice(h * T, (h + 1) * T)
        dqt = jnp.dot(kT[...], ds_ref[:, cols], preferred_element_type=f32)
        dq_ref[:, h * D : (h + 1) * D] = jnp.transpose(dqt).astype(bf16)

    def give(m, half):
        part = half_of[half]
        return remote(
            gb.at[2 * m + 1, part], pst.at[m, part], psend.at[2 + half, m], precv.at[2 + half, m], (partner, me)
        )

    quarter_of = [slice(e * T // 2, (e + 1) * T // 2) for e in range(4)]

    def xback(j, e):
        part = quarter_of[e]
        return remote(
            gb.at[2 * j, part], xst.at[j, part], xsend.at[2 + e, j], xrecv.at[2 + e, j], (chip(NX - j), me)
        )

    def zback(e):
        part = quarter_of[e]
        return remote(gb.at[8, part], zst.at[part], zsend.at[2 + e], zrecv.at[2 + e], (down, me))

    def odd(j, half):
        gb[j, half_of[half]] = gradient[half](j).astype(bf16)
        give(j // 2, half).start()

    def even(j, half):
        part = half_of[half]
        grad = gradient[half](j)
        for m in {4: (2, 1), 6: (3,), 2: (0,)}[j]:
            give(m, half).wait()
        gb[j, part] = (grad + pst[j // 2 - core, part].astype(f32)).astype(bf16)
        for e in (2 * half, 2 * half + 1):
            xback(j // 2, e).start()

    first_part = jnp.where(core == 0, 1.0, 0.0)
    last_part = jnp.where(core == 1, 1.0, 0.0)

    def fold(e):
        part = quarter_of[e]
        total = own[part] + pst[0, part].astype(f32) * first_part
        prev = pst[3, part].astype(f32) * last_part
        for j in (2, 3, 1):
            xback(j, e).wait()
            mine = jnp.where(x + j < NX, 1.0, 0.0)
            got = xst[j, part].astype(f32)
            total += got * mine
            prev += got * (1.0 - mine)
        gb[8, part] = prev.astype(bf16)
        pl.when(not_first)(zback(e).start)
        own[part] = total

    out = (kg, vg)

    def deliver(half, d):
        rows = pl.ds(pl.multiple_of(half * T + peer(d) * ROWS, ROWS), ROWS)
        return remote(
            fin.at[rows], out[half].at[:, own_col], asend.at[2 + half, d], arecv.at[2 + half, d], (i, peer(d))
        )

    def finish(e):
        part = quarter_of[e]
        half = e // 2
        pl.when(not_last)(zback(e).wait_recv)
        fin[part] = (own[part] + zst[part].astype(f32)).astype(bf16)
        for d in range(1, ND):
            here = lax.div(peer(d), ND // 2) == e % 2
            pl.when(here)(deliver(half, d).start)

    for j in (5, 3, 7, 1):
        odd(j, 1)
    for j in (4, 6, 2):
        even(j, 1)
    own[VALUES] = value_gradient(0)
    odd(5, 0)
    odd(3, 0)
    odd(7, 0)
    even(4, 0)
    odd(1, 0)
    even(6, 0)
    fold(2)
    fold(3)
    even(2, 0)
    own[KEYS] = key_gradient(0)
    for h in range(4):
        query_gradient(h)
    fold(0)
    fold(1)
    finish(2)
    finish(3)
    for h in range(4, 8):
        query_gradient(h)
    finish(0)
    finish(1)
    kg[:, own_col] = fin[own_row[0]]
    vg[:, own_col] = fin[own_row[1]]
    for e in range(4):
        pl.when(not_first)(zback(e).wait_send)
    for half in (1, 0):
        for d in range(1, ND):
            deliver(half, d).wait()
    dk_ref[...] = kg[...]
    dv_ref[...] = vg[...]


def write_kernel(o_in, dq_in, dk_in, dv_in, o_out, dq_out, dk_out, dv_out, sem):
    pairs = ((o_in, o_out), (dq_in, dq_out), (dk_in, dk_out), (dv_in, dv_out))
    copies = [pltpu.make_async_copy(a, b, sem.at[n]) for n, (a, b) in enumerate(pairs)]
    for copy in copies:
        copy.start()
    for copy in copies:
        copy.wait()


def body(queries, key_vectors, value_vectors, output_gradient, doc_lengths):
    vm = pl.BlockSpec(memory_space=pltpu.VMEM)
    free = pl.BlockSpec(memory_space=pl.ANY)
    dma = pltpu.SemaphoreType.DMA
    vmem = pltpu.VMEM
    big = jax.ShapeDtypeStruct((T, H * D), bf16)
    small = jax.ShapeDtypeStruct((ROWS, ND * D), bf16)
    arrays = [
        pltpu.with_memory_space_constraint(a, pltpu.HBM)
        for a in (doc_lengths.reshape(1, -1), queries, output_gradient, key_vectors, value_vectors)
    ]
    parts = pl.pallas_call(
        functools.partial(kernel, lax.axis_size("ctx")),
        out_shape=(big, big, small, small),
        in_specs=[free] * 5,
        out_specs=(vm,) * 4,
        scratch_shapes=[
            vmem((1, doc_lengths.shape[0]), jnp.int32),
            vmem((T, H * D), bf16),
            vmem((T, H * D), bf16),
            vmem((9, 2 * T, D), bf16),
            vmem((9, 2 * T, D), bf16),
            vmem((4, 2 * T, D), bf16),
            vmem((4, 2 * T, D), bf16),
            vmem((2 * T, D), bf16),
            vmem((2 * T, D), f32),
            vmem((2 * T, D), bf16),
            vmem((ROWS, ND * D), bf16),
            vmem((ROWS, ND * D), bf16),
            vmem((T, D), bf16),
            vmem((W * T, D), bf16),
            vmem((T, D), bf16),
            vmem((H * T, D), bf16),
            vmem((H * T, D), bf16),
            vmem((H * T, D), bf16),
            vmem((D, W * T), bf16),
            vmem((D + 16, W * T), bf16),
            vmem((8, H * T), f32),
            vmem((W * T, H * T), f32),
            vmem((W * T, H * T), bf16),
            vmem((W * T, H * T), bf16),
            dma((5,)),
            dma((4, ND)),
            dma((4, ND)),
            dma((6,)),
            dma((6,)),
            dma((6, NX)),
            dma((6, NX)),
            dma((4, 4)),
            dma((4, 4)),
        ],
        compiler_params=pltpu.CompilerParams(
            collective_id=0, has_side_effects=True, vmem_limit_bytes=52 << 20
        ),
        name="attention",
    )(*arrays)
    return pl.pallas_call(
        write_kernel,
        out_shape=(big, big, small, small),
        in_specs=[free] * 4,
        out_specs=(free,) * 4,
        scratch_shapes=[dma((4,))],
        compiler_params=pltpu.CompilerParams(vmem_limit_bytes=2 << 20),
        name="write",
    )(*parts)


def solution(mesh):
    return jax.shard_map(
        body,
        mesh=mesh,
        in_specs=(P("ctx", "tp"), P(("ctx", "tp"), None), P(("ctx", "tp"), None), P("ctx", "tp"), P()),
        out_specs=(P("ctx", "tp"), P("ctx", "tp"), P(("ctx", "tp"), None), P(("ctx", "tp"), None)),
        check_vma=False,
    )
```
